32 devices in a mesh: blk: 32 (over z, y, x, core), feat: 1.
Axes of the slice: x: 2, y: 2, z: 4, core: 2. Of those that a mesh axis runs over, the one named last changes fastest.
Arguments:
- activations: bfloat16 [5120, 4096], P('blk', 'feat'), may hold values from -6 to 6
- live_rows: int32 [32], replicated, may hold values from 1 to 160, as said below
- encoder_weight: bfloat16 [4096, 32768], P('feat', 'blk'), may hold values from -0.09375 to 0.09375
- encoder_bias: float32 [32768], P('blk'), may hold values from -3 to 3
- decoder_weight: bfloat16 [4, 1024, 32768], P(None, 'feat', 'blk'), may hold values from -0.09375 to 0.09375
- decoder_bias: float32 [32768], P('blk'), may hold values from -3 to 3
- targets: bfloat16 [640, 32768], P('feat', 'blk'), may hold values from -6 to 6
Outputs:
- reconstruction: float32 [640, 32768], P('feat', 'blk')
- decoder_grad: float32 [4, 1024, 32768], P(None, 'feat', 'blk')
The draws below stay inside these ranges and needn't reach their ends.
Inputs may be any that keep to these rules, and one draw needn't show every extreme that they name: `live_rows`: live rows of a block of 160 slots are its first ones; some block is full.
All inputs are finite; a program needn't handle non-finite values.
Results may differ from the reference program's by a relative error of at most 0.015.
Values may be sent and summed in bfloat16 or wider, within the bound.
A program may use at most 128 MiB of HBM per device.

```python
import jax
import jax.numpy as jnp
from jax import lax

D = 4096
F = 4096
G = 8
TOK_DEV = 160
OWN = 4
TOKG = 640
ROWS = 5120
N_BLK = 32
N_FEAT = 1


def draw_live_rows(key, part):
    blocks = ROWS // TOK_DEV
    counts = jax.random.randint(key, (blocks,), 1, TOK_DEV + 1)
    chosen = jax.random.randint(jax.random.fold_in(key, 7), (), 0, blocks)
    return counts.at[chosen].set(TOK_DEV).astype(jnp.int32)


def shard_levels(own_key, dims, split, smallest, top_value):
    def one(position, shards_of):
        steps = jax.random.uniform(jax.random.fold_in(jax.random.fold_in(own_key, 6), position), (shards_of,), jnp.float32, smallest / len(split), top_value / len(split))
        return jnp.repeat(jnp.exp(steps), dims[position] // shards_of).reshape((-1,) + (1,) * (len(dims) - position - 1))

    loudness = one(*split[0])
    for cut in split[1:]:
        loudness = loudness * one(*cut)
    return loudness


def gaussian(own_key, extent, scale, limit, shards=(), kind=jnp.bfloat16):
    entries = scale * jax.random.normal(own_key, extent, jnp.float32)
    if shards:
        entries = entries * shard_levels(own_key, extent, shards, -0.22, 0.18)
    return jnp.clip(entries, -limit, limit).astype(kind)


def setup_inputs(seed: int = 0) -> dict:
    keys = jax.random.split(jax.random.key(seed), 8)
    return {
        "activations": gaussian(keys[0], (ROWS, D), 1.0, 6.0, ((0, 32),)),
        "live_rows": draw_live_rows(jax.random.fold_in(keys[7], 71), 0),
        "encoder_weight": gaussian(keys[2], (D, G * F), D ** -0.5, 0.09375, ((1, 32),)),
        "encoder_bias": gaussian(keys[3], (G * F,), 0.5, 3.0, ((0, 32),), jnp.float32),
        "decoder_weight": gaussian(keys[4], (OWN, F // OWN, G * D), F ** -0.5, 0.09375, ((2, 32),)),
        "decoder_bias": gaussian(keys[5], (G * D,), 0.5, 3.0, ((0, 32),), jnp.float32),
        "targets": gaussian(keys[6], (TOKG, G * D), 1.0, 6.0, ((1, 32),)),
    }


def one_group(packed):
    inputs, live_mask, enc_block, enc_bias, dec_block, dec_bias, target_block = packed
    slab = D // N_FEAT
    row_count = inputs.shape[0]
    preact = jnp.zeros((row_count, F), jnp.float32)
    for share_index in range(N_FEAT):
        partial_value = jnp.dot(inputs[:, share_index * slab:(share_index + 1) * slab], enc_block[share_index * slab:(share_index + 1) * slab, :], preferred_element_type=jnp.float32)
        preact = preact + lax.optimization_barrier(partial_value.astype(jnp.bfloat16)).astype(jnp.float32)
    codes = (jax.nn.relu(preact + enc_bias[None, :]) * live_mask[:, None]).astype(jnp.bfloat16)
    owners = N_BLK // G
    per_share = F // owners // N_FEAT
    codes_split = codes.reshape(row_count, owners, N_FEAT, per_share)
    dec_split = dec_block.reshape(owners, N_FEAT, per_share, D)
    rebuilt = jnp.zeros((row_count, D), jnp.float32)
    for share_index in range(N_FEAT):
        left = codes_split[:, :, share_index, :].reshape(row_count, owners * per_share)
        right = dec_split[:, share_index].reshape(owners * per_share, D)
        partial_value = jnp.dot(left, right, preferred_element_type=jnp.float32)
        rebuilt = rebuilt + lax.optimization_barrier(partial_value.astype(jnp.bfloat16)).astype(jnp.float32)
    rebuilt = rebuilt + dec_bias[None, :]
    residual = ((rebuilt - target_block.astype(jnp.float32)) * live_mask[:, None]).astype(jnp.bfloat16)
    gradient = jnp.dot(codes.T, residual, preferred_element_type=jnp.float32)
    return rebuilt, gradient


def reference(activations, live_rows, encoder_weight, encoder_bias, decoder_weight, decoder_bias, targets):
    owners = N_BLK // G
    positions = jnp.arange(TOK_DEV, dtype=jnp.int32)
    live_mask = (positions[None, :] < live_rows[:, None]).astype(jnp.float32).reshape(G, TOKG)
    inputs = activations.reshape(G, TOKG, D)
    enc_blocks = encoder_weight.reshape(D, G, F).transpose(1, 0, 2)
    enc_biases = encoder_bias.reshape(G, F)
    dec_blocks = decoder_weight.reshape(owners, F // owners, G, D).transpose(2, 0, 1, 3).reshape(G, F, D)
    dec_biases = decoder_bias.reshape(G, D)
    target_blocks = targets.reshape(TOKG, G, D).transpose(1, 0, 2)
    rebuilt, gradient = lax.map(one_group, (inputs, live_mask, enc_blocks, enc_biases, dec_blocks, dec_biases, target_blocks))
    reconstruction = rebuilt.transpose(1, 0, 2).reshape(TOKG, G * D)
    decoder_grad = gradient.reshape(G, owners, F // owners, D).transpose(1, 2, 0, 3).reshape(owners, F // owners, G * D)
    return reconstruction, decoder_grad
```

```python
import functools

import jax
import jax.numpy as jnp
from jax import lax
from jax.experimental import pallas as pl
from jax.experimental.pallas import tpu as pltpu
from jax.sharding import PartitionSpec as P

G = 8
MESH = pl.DeviceIdType.MESH


def cuts(rows, parts):
    if rows % 16 or rows // 16 < len(parts):
        return [(0, rows)]
    tiles, total, edges = rows // 16, sum(parts), [0]
    for k in range(1, len(parts)):
        edges.append(max(edges[-1] + 1, tiles * sum(parts[:k]) // total))
    edges.append(tiles)
    return [(16 * a, 16 * (b - a)) for a, b in zip(edges[:-1], edges[1:])]


def gather_kernel(
    act_cuts,
    code_cuts,
    act_hbm,
    live_hbm,
    enc_hbm,
    bias_hbm,
    dec_hbm,
    dec_bias_hbm,
    targets_hbm,
    codes,
    residual,
    rebuilt,
    acts,
    enc,
    dec,
    part,
    targets,
    live_ref,
    bias_ref,
    dec_bias_ref,
    load_sem,
    s1_send,
    s1_recv,
    s2_send,
    s2_recv,
    s3_send,
    s3_recv,
    t1_send,
    t1_recv,
    t2_send,
    t2_recv,
    t3_send,
    t3_recv,
):
    position = lax.axis_index("blk")
    share = lax.axis_index("feat")
    base = position // 4 * 4
    me = position % 4
    core = me % 2
    home = me - core
    away = 2 - home
    twin = home + 1 - core
    peer = away + core
    peer_twin = away + 1 - core
    on_chip = (base + twin, share)
    across = (base + peer, share)

    rows = acts.shape[1]
    width = enc.shape[1]
    tile = min(256, width)
    tiles = width // tile

    load_act = pltpu.make_async_copy(act_hbm, acts.at[me], load_sem.at[0])
    load_enc = pltpu.make_async_copy(enc_hbm, enc, load_sem.at[1])
    load_dec = pltpu.make_async_copy(dec_hbm, dec, load_sem.at[2])
    load_targets = pltpu.make_async_copy(targets_hbm, targets, load_sem.at[3])
    load_live = pltpu.make_async_copy(live_hbm, live_ref, load_sem.at[4])
    load_bias = pltpu.make_async_copy(bias_hbm, bias_ref, load_sem.at[5])
    load_dec_bias = pltpu.make_async_copy(dec_bias_hbm, dec_bias_ref, load_sem.at[6])
    load_live.start()
    load_bias.start()
    load_act.start()
    load_enc.start()
    load_dec_bias.start()

    barrier = pltpu.get_barrier_semaphore()
    for neighbour in (on_chip, across):
        pl.semaphore_signal(barrier, inc=1, device_id=neighbour, device_id_type=MESH)
    pl.semaphore_wait(barrier, 2)

    def remote(src, dst, send, recv, to):
        return pltpu.make_async_remote_copy(
            src_ref=src,
            dst_ref=dst,
            send_sem=send,
            recv_sem=recv,
            device_id=to,
            device_id_type=MESH,
        )

    def s1(b):
        return remote(act_hbm, acts.at[b], s1_send.at[0], s1_recv.at[0], on_chip)

    def s2(b, h):
        at = pl.ds(*act_cuts[h])
        return remote(act_hbm.at[at], acts.at[b, at], s2_send.at[h], s2_recv.at[h], across)

    def s3(b, h):
        ref = acts.at[b, pl.ds(*act_cuts[h])]
        return remote(ref, ref, s3_send.at[h], s3_recv.at[h], on_chip)

    def at_rows(b, start, count):
        return pl.ds(pl.multiple_of(b * rows + start, count if rows % 16 else 16), count)

    def t1(f, b):
        ref = codes.at[f, at_rows(b, 0, rows)]
        return remote(ref, ref, t1_send.at[b], t1_recv.at[b], on_chip)

    def t2(f, b, h):
        ref = codes.at[f, at_rows(b, *code_cuts[h])]
        return remote(ref, ref, t2_send.at[b, h], t2_recv.at[b, h], across)

    def t3(f, b, h):
        ref = codes.at[f, at_rows(b, *code_cuts[h])]
        return remote(ref, ref, t3_send.at[b, h], t3_recv.at[b, h], on_chip)

    every = range(len(code_cuts))
    for h in range(len(act_cuts)):
        s2(me, h).start()
    s1(me).start()
    load_dec.start()
    load_targets.start()

    def encode(b):
        live = live_ref[base + b]
        keep = lax.broadcasted_iota(jnp.int32, (rows, tile), 0) < live

        def column(n, carry):
            at = pl.ds(pl.multiple_of(n * tile, tile), tile)
            product = jnp.dot(acts[b], enc[:, at], preferred_element_type=jnp.float32)
            value = product.astype(jnp.bfloat16).astype(jnp.float32) + bias_ref[:, at]
            value = jnp.where(keep, jnp.maximum(value, 0.0), 0.0)
            codes[me, at_rows(b, 0, rows), at] = value.astype(jnp.bfloat16)
            return carry

        lax.fori_loop(0, tiles, column, 0)

    def home_features(b):
        here = at_rows(b, 0, rows)

        def column(n, carry):
            at = pl.ds(pl.multiple_of(n * tile, tile), tile)
            first = jnp.dot(
                codes[me, here], dec[me, :, at], preferred_element_type=jnp.float32
            )
            second = jnp.dot(
                codes[twin, here], dec[twin, :, at], preferred_element_type=jnp.float32
            )
            part[here, at] = first + second
            return carry

        lax.fori_loop(0, tiles, column, 0)

    def finish(b, h):
        start, count = code_cuts[h]
        here = at_rows(b, start, count)
        t2(peer, b, h).wait_recv()
        t3(peer, b, h).start()
        part[here] += jnp.dot(codes[peer, here], dec[peer], preferred_element_type=jnp.float32)
        t3(peer_twin, b, h).wait_recv()
        whole = part[here] + jnp.dot(
            codes[peer_twin, here], dec[peer_twin], preferred_element_type=jnp.float32
        )
        whole = whole.astype(jnp.bfloat16).astype(jnp.float32) + dec_bias_ref[...]
        rebuilt[here] = whole
        row = start + lax.broadcasted_iota(jnp.int32, whole.shape, 0)
        error = whole - targets[here].astype(jnp.float32)
        residual[here] = jnp.where(row < live_ref[base + b], error, 0.0).astype(jnp.bfloat16)

    load_live.wait()
    load_bias.wait()
    load_act.wait()
    load_enc.wait()
    encode(me)
    t1(me, me).start()
    s1(twin).wait_recv()
    encode(twin)
    t1(me, twin).start()
    load_dec.wait()
    load_targets.wait()
    load_dec_bias.wait()
    t1(twin, home).wait_recv()
    t1(twin, home + 1).wait_recv()

    def home_step(i, carry):
        home_features(home + i)
        return carry

    lax.fori_loop(0, 2, home_step, 0)

    for h in range(len(act_cuts)):
        s2(peer, h).wait_recv()
        s3(peer, h).start()
    for h in range(len(act_cuts)):
        s2(me, h).wait_send()
    for b in (home, home + 1):
        for h in every:
            t2(me, b, h).start()
    encode(peer)
    t1(me, peer).start()
    for h in range(len(act_cuts)):
        s3(peer_twin, h).wait_recv()
    encode(peer_twin)
    t1(me, peer_twin).start()
    for b in (away, away + 1):
        for h in every:
            t2(me, b, h).start()
    t1(twin, away).wait_recv()
    t1(twin, away + 1).wait_recv()

    def away_step(i, carry):
        home_features(away + i)
        return carry

    lax.fori_loop(0, 2, away_step, 0)

    def finish_step(i, carry):
        for h in every:
            finish(lax.rem(away + i, 4), h)
        return carry

    lax.fori_loop(0, 4, finish_step, 0)

    s1(me).wait_send()
    for h in range(len(act_cuts)):
        s3(peer, h).wait_send()
    for b in range(4):
        t1(me, b).wait_send()
        for h in every:
            t2(me, b, h).wait_send()
            t3(peer, b, h).wait_send()


def gradient_kernel(span, codes_ref, residual_ref, rebuilt_ref, rebuilt_hbm, grad_hbm, grad, sem):
    owners, width = codes_ref.shape[0], codes_ref.shape[2]
    per = width // span
    copies = [pltpu.make_async_copy(rebuilt_ref, rebuilt_hbm, sem.at[owners * per])]
    copies[0].start()
    for i in range(owners * per):
        at = pl.ds(i % per * span, span)
        grad[i // per, at] = lax.dot_general(
            codes_ref[i // per, :, at],
            residual_ref[...],
            (((0,), (0,)), ((), ())),
            preferred_element_type=jnp.float32,
        )
        copy = pltpu.make_async_copy(grad.at[i // per, at], grad_hbm.at[i // per, at], sem.at[i])
        copy.start()
        copies.append(copy)
    for copy in copies:
        copy.wait()


def four_owners(
    activations, live_rows, encoder_weight, encoder_bias, decoder_weight, decoder_bias, targets
):
    rows, depth = activations.shape
    features = encoder_weight.shape[1]
    width = decoder_weight.shape[2]
    tokens = targets.shape[0]
    act_cuts = cuts(rows, (1, 1))
    code_cuts = cuts(rows, (5, 3, 2))
    any_space = pl.BlockSpec(memory_space=pl.ANY)
    stay = functools.partial(pltpu.with_memory_space_constraint, memory_space=pltpu.HBM)
    in_vmem = pl.BlockSpec(memory_space=pltpu.VMEM)
    in_hbm = pl.BlockSpec(memory_space=pltpu.HBM)
    dma = pltpu.SemaphoreType.DMA
    bf16 = jnp.bfloat16
    codes, residual, rebuilt = pl.pallas_call(
        functools.partial(gather_kernel, act_cuts, code_cuts),
        out_shape=(
            pltpu.VMEM((4, tokens, features), bf16),
            pltpu.VMEM((tokens, width), bf16),
            pltpu.VMEM((tokens, width), jnp.float32),
        ),
        in_specs=[in_hbm] * 7,
        out_specs=(in_vmem, in_vmem, in_vmem),
        scratch_shapes=[
            pltpu.VMEM((4, rows, depth), bf16),
            pltpu.VMEM((depth, features), bf16),
            pltpu.VMEM((4, features, width), bf16),
            pltpu.VMEM((tokens, width), jnp.float32),
            pltpu.VMEM((tokens, width), bf16),
            pltpu.SMEM(live_rows.shape, jnp.int32),
            pltpu.VMEM((1, features), jnp.float32),
            pltpu.VMEM((1, width), jnp.float32),
            dma((7,)),
            dma((1,)),
            dma((1,)),
            dma((len(act_cuts),)),
            dma((len(act_cuts),)),
            dma((len(act_cuts),)),
            dma((len(act_cuts),)),
            dma((4,)),
            dma((4,)),
            dma((4, len(code_cuts))),
            dma((4, len(code_cuts))),
            dma((4, len(code_cuts))),
            dma((4, len(code_cuts))),
        ],
        compiler_params=pltpu.CompilerParams(
            collective_id=0, has_side_effects=True, vmem_limit_bytes=44 * 1024 * 1024
        ),
        name="gather_codes",
    )(
        activations,
        stay(live_rows),
        encoder_weight,
        stay(encoder_bias[None, :]),
        decoder_weight,
        stay(decoder_bias[None, :]),
        targets,
    )

    span = min(256, features)
    rebuilt, grad = pl.pallas_call(
        functools.partial(gradient_kernel, span),
        out_shape=(
            jax.ShapeDtypeStruct((tokens, width), jnp.float32),
            jax.ShapeDtypeStruct((4, features, width), jnp.float32),
        ),
        in_specs=[in_vmem, in_vmem, in_vmem],
        out_specs=(any_space, any_space),
        scratch_shapes=[
            pltpu.VMEM((4, features, width), jnp.float32),
            dma((4 * (features // span) + 1,)),
        ],
        compiler_params=pltpu.CompilerParams(vmem_limit_bytes=44 * 1024 * 1024),
        name="gradient",
    )(codes, residual, rebuilt)
    return rebuilt, grad


def from_partner(shard, axis, distance):
    return lax.ppermute(shard, axis, [(i, i ^ 1 << distance) for i in range(lax.axis_size(axis))])


def group_rows(block, levels, position):
    for bit in range(levels):
        other = from_partner(block, "blk", bit)
        upper = position >> bit & 1 == 1
        block = jnp.where(
            upper, jnp.concatenate([other, block], 0), jnp.concatenate([block, other], 0)
        )
    return block


def general(
    activations, live_rows, encoder_weight, encoder_bias, decoder_weight, decoder_bias, targets
):
    owners = lax.axis_size("blk") // G
    levels = owners.bit_length() - 1
    shares = lax.axis_size("feat")
    position = lax.axis_index("blk")
    share_index = lax.axis_index("feat")
    group_index = position // owners
    tok_rows = activations.shape[0]
    counts = lax.dynamic_slice_in_dim(live_rows, group_index * owners, owners)
    positions = jnp.arange(tok_rows, dtype=jnp.int32)
    live_mask = (positions[None, :] < counts[:, None]).astype(jnp.float32).reshape(-1)
    gathered = group_rows(activations, levels, position)
    per_share = encoder_weight.shape[1] // shares
    bias_share = lax.dynamic_slice_in_dim(encoder_bias, share_index * per_share, per_share)
    columns = encoder_weight
    whole = lax.psum(
        lax.dot_general(
            columns, gathered, (((0,), (1,)), ((), ())), preferred_element_type=jnp.float32
        ).astype(jnp.bfloat16),
        "feat",
    ).astype(jnp.float32)
    preact = lax.dynamic_slice_in_dim(whole, share_index * per_share, per_share, 0)
    codes_by_feature = (jax.nn.relu(preact + bias_share[:, None]) * live_mask[None, :]).astype(
        jnp.bfloat16
    )
    codes_all = group_rows(codes_by_feature, levels, position)
    decoder_rows = decoder_weight.reshape(-1, decoder_weight.shape[2])
    block_rows = gathered.shape[0] // shares
    columns = codes_all
    summed = lax.psum_scatter(
        lax.dot_general(
            columns, decoder_rows, (((0,), (0,)), ((), ())), preferred_element_type=jnp.float32
        ).astype(jnp.bfloat16),
        "feat",
        scatter_dimension=0,
        tiled=True,
    ).astype(jnp.float32)
    rebuilt = summed + decoder_bias[None, :]
    mask_block = lax.dynamic_slice_in_dim(live_mask, share_index * block_rows, block_rows)
    residual = ((rebuilt - targets.astype(jnp.float32)) * mask_block[:, None]).astype(jnp.bfloat16)
    columns = codes_all
    gradient = jnp.dot(
        columns,
        lax.all_gather(residual, "feat", axis=0, tiled=True),
        preferred_element_type=jnp.float32,
    )
    return (rebuilt, gradient.reshape(decoder_weight.shape))


def solution(mesh):
    in_specs = (
        P("blk", "feat"),
        P(),
        P("feat", "blk"),
        P("blk"),
        P(None, "feat", "blk"),
        P("blk"),
        P("feat", "blk"),
    )
    out_specs = (P("feat", "blk"), P(None, "feat", "blk"))
    fused = mesh.shape["blk"] // G == 4 and mesh.shape["feat"] == 1
    return jax.shard_map(
        four_owners if fused else general,
        mesh=mesh,
        in_specs=in_specs,
        out_specs=out_specs,
        check_vma=False,
    )
```

```python
import functools

import jax
import jax.numpy as jnp
from jax import lax
from jax.experimental import pallas as pl
from jax.experimental.pallas import tpu as pltpu
from jax.sharding import PartitionSpec as P

G = 8
MESH = pl.DeviceIdType.MESH


def cuts(rows, parts):
    if rows % 16 or rows // 16 < len(parts):
        return [(0, rows)]
    tiles, total, edges = rows // 16, sum(parts), [0]
    for k in range(1, len(parts)):
        edges.append(max(edges[-1] + 1, tiles * sum(parts[:k]) // total))
    edges.append(tiles)
    return [(16 * a, 16 * (b - a)) for a, b in zip(edges[:-1], edges[1:])]


def gather_kernel(
    act_cuts,
    code_cuts,
    act_hbm,
    live_hbm,
    enc_hbm,
    bias_hbm,
    dec_hbm,
    dec_bias_hbm,
    targets_hbm,
    codes,
    residual,
    rebuilt,
    acts,
    enc,
    dec,
    part,
    targets,
    live_ref,
    bias_ref,
    dec_bias_ref,
    load_sem,
    s1_send,
    s1_recv,
    s2_send,
    s2_recv,
    s3_send,
    s3_recv,
    t1_send,
    t1_recv,
    t2_send,
    t2_recv,
    t3_send,
    t3_recv,
):
    position = lax.axis_index("blk")
    share = lax.axis_index("feat")
    base = position // 4 * 4
    me = position % 4
    core = me % 2
    home = me - core
    away = 2 - home
    twin = home + 1 - core
    peer = away + core
    peer_twin = away + 1 - core
    on_chip = (base + twin, share)
    across = (base + peer, share)

    rows = acts.shape[1]
    width = enc.shape[1]
    tile = min(256, width)
    tiles = width // tile

    load_act = pltpu.make_async_copy(act_hbm, acts.at[me], load_sem.at[0])
    load_enc = pltpu.make_async_copy(enc_hbm, enc, load_sem.at[1])
    load_dec = pltpu.make_async_copy(dec_hbm, dec, load_sem.at[2])
    load_targets = pltpu.make_async_copy(targets_hbm, targets, load_sem.at[3])
    load_live = pltpu.make_async_copy(live_hbm, live_ref, load_sem.at[4])
    load_bias = pltpu.make_async_copy(bias_hbm, bias_ref, load_sem.at[5])
    load_dec_bias = pltpu.make_async_copy(dec_bias_hbm, dec_bias_ref, load_sem.at[6])
    load_live.start()
    load_bias.start()
    load_act.start()
    load_enc.start()
    load_dec_bias.start()

    barrier = pltpu.get_barrier_semaphore()
    for neighbour in (on_chip, across):
        pl.semaphore_signal(barrier, inc=1, device_id=neighbour, device_id_type=MESH)
    pl.semaphore_wait(barrier, 2)

    def remote(src, dst, send, recv, to):
        return pltpu.make_async_remote_copy(
            src_ref=src,
            dst_ref=dst,
            send_sem=send,
            recv_sem=recv,
            device_id=to,
            device_id_type=MESH,
        )

    def s1(b):
        return remote(act_hbm, acts.at[b], s1_send.at[0], s1_recv.at[0], on_chip)

    def s2(b, h):
        at = pl.ds(*act_cuts[h])
        return remote(act_hbm.at[at], acts.at[b, at], s2_send.at[h], s2_recv.at[h], across)

    def s3(b, h):
        ref = acts.at[b, pl.ds(*act_cuts[h])]
        return remote(ref, ref, s3_send.at[h], s3_recv.at[h], on_chip)

    def at_rows(b, start, count):
        return pl.ds(pl.multiple_of(b * rows + start, count if rows % 16 else 16), count)

    def t1(f, b):
        ref = codes.at[f, at_rows(b, 0, rows)]
        return remote(ref, ref, t1_send.at[b], t1_recv.at[b], on_chip)

    def t2(f, b, h):
        ref = codes.at[f, at_rows(b, *code_cuts[h])]
        return remote(ref, ref, t2_send.at[b, h], t2_recv.at[b, h], across)

    def t3(f, b, h):
        ref = codes.at[f, at_rows(b, *code_cuts[h])]
        return remote(ref, ref, t3_send.at[b, h], t3_recv.at[b, h], on_chip)

    every = range(len(code_cuts))
    for h in range(len(act_cuts)):
        s2(me, h).start()
    s1(me).start()
    load_dec.start()
    load_targets.start()

    def encode(b):
        live = live_ref[base + b]
        keep = lax.broadcasted_iota(jnp.int32, (rows, tile), 0) < live

        def column(n, carry):
            at = pl.ds(pl.multiple_of(n * tile, tile), tile)
            product = jnp.dot(acts[b], enc[:, at], preferred_element_type=jnp.float32)
            value = product.astype(jnp.bfloat16).astype(jnp.float32) + bias_ref[:, at]
            value = jnp.where(keep, jnp.maximum(value, 0.0), 0.0)
            codes[me, at_rows(b, 0, rows), at] = value.astype(jnp.bfloat16)
            return carry

        lax.fori_loop(0, tiles, column, 0)

    def home_features(b):
        here = at_rows(b, 0, rows)

        def column(n, carry):
            at = pl.ds(pl.multiple_of(n * tile, tile), tile)
            first = jnp.dot(
                codes[me, here], dec[me, :, at], preferred_element_type=jnp.float32
            )
            second = jnp.dot(
                codes[twin, here], dec[twin, :, at], preferred_element_type=jnp.float32
            )
            part[here, at] = first + second
            return carry

        lax.fori_loop(0, tiles, column, 0)

    def finish(b, h):
        start, count = code_cuts[h]
        here = at_rows(b, start, count)
        t2(peer, b, h).wait_recv()
        t3(peer, b, h).start()
        part[here] += jnp.dot(codes[peer, here], dec[peer], preferred_element_type=jnp.float32)
        t3(peer_twin, b, h).wait_recv()
        whole = part[here] + jnp.dot(
            codes[peer_twin, here], dec[peer_twin], preferred_element_type=jnp.float32
        )
        whole = whole.astype(jnp.bfloat16).astype(jnp.float32) + dec_bias_ref[...]
        rebuilt[here] = whole
        row = start + lax.broadcasted_iota(jnp.int32, whole.shape, 0)
        error = whole - targets[here].astype(jnp.float32)
        residual[here] = jnp.where(row < live_ref[base + b], error, 0.0).astype(jnp.bfloat16)

    load_live.wait()
    load_bias.wait()
    load_act.wait()
    load_enc.wait()
    encode(me)
    t1(me, me).start()
    s1(twin).wait_recv()
    encode(twin)
    t1(me, twin).start()
    for b in (home, home + 1):
        for h in every:
            t2(me, b, h).start()
    load_dec.wait()
    load_targets.wait()
    load_dec_bias.wait()
    t1(twin, home).wait_recv()
    t1(twin, home + 1).wait_recv()

    def home_step(i, carry):
        home_features(home + i)
        return carry

    lax.fori_loop(0, 2, home_step, 0)

    for h in range(len(act_cuts)):
        s2(peer, h).wait_recv()
        s3(peer, h).start()
    encode(peer)
    t1(me, peer).start()
    for h in range(len(act_cuts)):
        s3(peer_twin, h).wait_recv()
    encode(peer_twin)
    t1(me, peer_twin).start()
    for b in (away, away + 1):
        for h in every:
            t2(me, b, h).start()
    t1(twin, away).wait_recv()
    t1(twin, away + 1).wait_recv()

    def away_step(i, carry):
        home_features(away + i)
        return carry

    lax.fori_loop(0, 2, away_step, 0)

    def finish_step(i, carry):
        for h in every:
            finish(lax.rem(away + i, 4), h)
        return carry

    lax.fori_loop(0, 4, finish_step, 0)

    s1(me).wait_send()
    for h in range(len(act_cuts)):
        s2(me, h).wait_send()
    for h in range(len(act_cuts)):
        s3(peer, h).wait_send()
    for b in range(4):
        t1(me, b).wait_send()
        for h in every:
            t2(me, b, h).wait_send()
            t3(peer, b, h).wait_send()


def gradient_kernel(span, codes_ref, residual_ref, rebuilt_ref, rebuilt_hbm, grad_hbm, grad, sem):
    owners, width = codes_ref.shape[0], codes_ref.shape[2]
    per = width // span
    copies = [pltpu.make_async_copy(rebuilt_ref, rebuilt_hbm, sem.at[owners * per])]
    copies[0].start()
    for i in range(owners * per):
        at = pl.ds(i % per * span, span)
        grad[i // per, at] = lax.dot_general(
            codes_ref[i // per, :, at],
            residual_ref[...],
            (((0,), (0,)), ((), ())),
            preferred_element_type=jnp.float32,
        )
        copy = pltpu.make_async_copy(grad.at[i // per, at], grad_hbm.at[i // per, at], sem.at[i])
        copy.start()
        copies.append(copy)
    for copy in copies:
        copy.wait()


def four_owners(
    activations, live_rows, encoder_weight, encoder_bias, decoder_weight, decoder_bias, targets
):
    rows, depth = activations.shape
    features = encoder_weight.shape[1]
    width = decoder_weight.shape[2]
    tokens = targets.shape[0]
    act_cuts = cuts(rows, (1, 1))
    code_cuts = cuts(rows, (5, 3, 2))
    any_space = pl.BlockSpec(memory_space=pl.ANY)
    stay = functools.partial(pltpu.with_memory_space_constraint, memory_space=pltpu.HBM)
    in_vmem = pl.BlockSpec(memory_space=pltpu.VMEM)
    in_hbm = pl.BlockSpec(memory_space=pltpu.HBM)
    dma = pltpu.SemaphoreType.DMA
    bf16 = jnp.bfloat16
    codes, residual, rebuilt = pl.pallas_call(
        functools.partial(gather_kernel, act_cuts, code_cuts),
        out_shape=(
            pltpu.VMEM((4, tokens, features), bf16),
            pltpu.VMEM((tokens, width), bf16),
            pltpu.VMEM((tokens, width), jnp.float32),
        ),
        in_specs=[in_hbm] * 7,
        out_specs=(in_vmem, in_vmem, in_vmem),
        scratch_shapes=[
            pltpu.VMEM((4, rows, depth), bf16),
            pltpu.VMEM((depth, features), bf16),
            pltpu.VMEM((4, features, width), bf16),
            pltpu.VMEM((tokens, width), jnp.float32),
            pltpu.VMEM((tokens, width), bf16),
            pltpu.SMEM(live_rows.shape, jnp.int32),
            pltpu.VMEM((1, features), jnp.float32),
            pltpu.VMEM((1, width), jnp.float32),
            dma((7,)),
            dma((1,)),
            dma((1,)),
            dma((len(act_cuts),)),
            dma((len(act_cuts),)),
            dma((len(act_cuts),)),
            dma((len(act_cuts),)),
            dma((4,)),
            dma((4,)),
            dma((4, len(code_cuts))),
            dma((4, len(code_cuts))),
            dma((4, len(code_cuts))),
            dma((4, len(code_cuts))),
        ],
        compiler_params=pltpu.CompilerParams(
            collective_id=0, has_side_effects=True, vmem_limit_bytes=44 * 1024 * 1024
        ),
        name="gather_codes",
    )(
        activations,
        stay(live_rows),
        encoder_weight,
        stay(encoder_bias[None, :]),
        decoder_weight,
        stay(decoder_bias[None, :]),
        targets,
    )

    span = min(256, features)
    rebuilt, grad = pl.pallas_call(
        functools.partial(gradient_kernel, span),
        out_shape=(
            jax.ShapeDtypeStruct((tokens, width), jnp.float32),
            jax.ShapeDtypeStruct((4, features, width), jnp.float32),
        ),
        in_specs=[in_vmem, in_vmem, in_vmem],
        out_specs=(any_space, any_space),
        scratch_shapes=[
            pltpu.VMEM((4, features, width), jnp.float32),
            dma((4 * (features // span) + 1,)),
        ],
        compiler_params=pltpu.CompilerParams(vmem_limit_bytes=44 * 1024 * 1024),
        name="gradient",
    )(codes, residual, rebuilt)
    return rebuilt, grad


def from_partner(shard, axis, distance):
    return lax.ppermute(shard, axis, [(i, i ^ 1 << distance) for i in range(lax.axis_size(axis))])


def group_rows(block, levels, position):
    for bit in range(levels):
        other = from_partner(block, "blk", bit)
        upper = position >> bit & 1 == 1
        block = jnp.where(
            upper, jnp.concatenate([other, block], 0), jnp.concatenate([block, other], 0)
        )
    return block


def general(
    activations, live_rows, encoder_weight, encoder_bias, decoder_weight, decoder_bias, targets
):
    owners = lax.axis_size("blk") // G
    levels = owners.bit_length() - 1
    shares = lax.axis_size("feat")
    position = lax.axis_index("blk")
    share_index = lax.axis_index("feat")
    group_index = position // owners
    tok_rows = activations.shape[0]
    counts = lax.dynamic_slice_in_dim(live_rows, group_index * owners, owners)
    positions = jnp.arange(tok_rows, dtype=jnp.int32)
    live_mask = (positions[None, :] < counts[:, None]).astype(jnp.float32).reshape(-1)
    gathered = group_rows(activations, levels, position)
    per_share = encoder_weight.shape[1] // shares
    bias_share = lax.dynamic_slice_in_dim(encoder_bias, share_index * per_share, per_share)
    columns = encoder_weight
    whole = lax.psum(
        lax.dot_general(
            columns, gathered, (((0,), (1,)), ((), ())), preferred_element_type=jnp.float32
        ).astype(jnp.bfloat16),
        "feat",
    ).astype(jnp.float32)
    preact = lax.dynamic_slice_in_dim(whole, share_index * per_share, per_share, 0)
    codes_by_feature = (jax.nn.relu(preact + bias_share[:, None]) * live_mask[None, :]).astype(
        jnp.bfloat16
    )
    codes_all = group_rows(codes_by_feature, levels, position)
    decoder_rows = decoder_weight.reshape(-1, decoder_weight.shape[2])
    block_rows = gathered.shape[0] // shares
    columns = codes_all
    summed = lax.psum_scatter(
        lax.dot_general(
            columns, decoder_rows, (((0,), (0,)), ((), ())), preferred_element_type=jnp.float32
        ).astype(jnp.bfloat16),
        "feat",
        scatter_dimension=0,
        tiled=True,
    ).astype(jnp.float32)
    rebuilt = summed + decoder_bias[None, :]
    mask_block = lax.dynamic_slice_in_dim(live_mask, share_index * block_rows, block_rows)
    residual = ((rebuilt - targets.astype(jnp.float32)) * mask_block[:, None]).astype(jnp.bfloat16)
    columns = codes_all
    gradient = jnp.dot(
        columns,
        lax.all_gather(residual, "feat", axis=0, tiled=True),
        preferred_element_type=jnp.float32,
    )
    return (rebuilt, gradient.reshape(decoder_weight.shape))


def solution(mesh):
    in_specs = (
        P("blk", "feat"),
        P(),
        P("feat", "blk"),
        P("blk"),
        P(None, "feat", "blk"),
        P("blk"),
        P("feat", "blk"),
    )
    out_specs = (P("feat", "blk"), P(None, "feat", "blk"))
    fused = mesh.shape["blk"] // G == 4 and mesh.shape["feat"] == 1
    return jax.shard_map(
        four_owners if fused else general,
        mesh=mesh,
        in_specs=in_specs,
        out_specs=out_specs,
        check_vma=False,
    )
```

```python
import functools

import jax
import jax.numpy as jnp
from jax import lax
from jax.experimental import pallas as pl
from jax.experimental.pallas import tpu as pltpu
from jax.sharding import PartitionSpec as P

G = 8
TILE = 16
MESH = pl.DeviceIdType.MESH


def cuts(rows, parts):
    if rows % 16 or rows // 16 < len(parts):
        return [(0, rows)]
    tiles, total, edges = rows // 16, sum(parts), [0]
    for k in range(1, len(parts)):
        edges.append(max(edges[-1] + 1, tiles * sum(parts[:k]) // total))
    edges.append(tiles)
    return [(16 * a, 16 * (b - a)) for a, b in zip(edges[:-1], edges[1:])]


def pieces_of(early, rest):
    first = [(0, *cut) for cut in cuts(early, (1, 1))]
    if rest:
        return first + [(1, 0, early)] + [(2, *cut) for cut in cuts(rest, (5, 3, 2))]
    return first + [(1, *cut) for cut in cuts(early, (5, 3, 2))]


def step(count):
    return jnp.clip(count, 0, 1)


def tile_of(first_live, second_live, tiles, k):
    first = first_live + TILE - 1 >> 4
    second = second_live + TILE - 1 >> 4
    late = 1 - step(first - k)
    inside = jnp.minimum(k - late * first, tiles - 1)
    live = first_live + late * (second_live - first_live) - TILE * inside
    return inside + late * tiles, step(first + second - k) * live


def gather_kernel(
    act_cuts,
    early,
    pieces,
    act_hbm,
    live_hbm,
    enc_hbm,
    bias_hbm,
    dec_hbm,
    dec_bias_hbm,
    targets_hbm,
    codes,
    residual,
    summed,
    acts_home,
    acts_away,
    packed,
    enc,
    dec,
    part,
    targets,
    packed_targets,
    keep,
    live_ref,
    bias_ref,
    dec_bias_ref,
    load_sem,
    s1_send,
    s1_recv,
    s2_send,
    s2_recv,
    s3_send,
    s3_recv,
    t1_send,
    t1_recv,
    t2_send,
    t2_recv,
    t3_send,
    t3_recv,
):
    position = lax.axis_index("blk")
    share = lax.axis_index("feat")
    base = position // 4 * 4
    me = position % 4
    core = me % 2
    home = me - core
    away = 2 - home
    chip = home // 2
    other = 1 - chip
    twin = home + 1 - core
    peer = away + core
    peer_twin = away + 1 - core
    on_chip = (base + twin, share)
    across = (base + peer, share)

    block_tiles = act_hbm.shape[0]
    total = codes.shape[1]
    rest = total - 2 * early
    width = enc.shape[1]
    column_tile = min(256, width)
    columns = width // column_tile

    def own_tiles(at_core, start, count):
        return pl.ds(at_core * block_tiles + start, count)

    load_act = pltpu.make_async_copy(
        act_hbm, acts_home.at[own_tiles(core, 0, block_tiles)], load_sem.at[0]
    )
    load_enc = pltpu.make_async_copy(enc_hbm, enc, load_sem.at[1])
    load_dec = pltpu.make_async_copy(dec_hbm, dec, load_sem.at[2])
    load_targets = pltpu.make_async_copy(targets_hbm, targets, load_sem.at[3])
    load_live = pltpu.make_async_copy(live_hbm, live_ref, load_sem.at[4])
    load_bias = pltpu.make_async_copy(bias_hbm, bias_ref, load_sem.at[5])
    load_dec_bias = pltpu.make_async_copy(dec_bias_hbm, dec_bias_ref, load_sem.at[6])
    load_live.start()
    load_bias.start()
    load_act.start()
    load_enc.start()
    load_dec_bias.start()

    barrier = pltpu.get_barrier_semaphore()
    for neighbour in (on_chip, across):
        pl.semaphore_signal(barrier, inc=1, device_id=neighbour, device_id_type=MESH)
    pl.semaphore_wait(barrier, 2)

    def remote(src, dst, send, recv, to):
        return pltpu.make_async_remote_copy(
            src_ref=src,
            dst_ref=dst,
            send_sem=send,
            recv_sem=recv,
            device_id=to,
            device_id_type=MESH,
        )

    def s1(at_core):
        ref = acts_home.at[own_tiles(at_core, 0, block_tiles)]
        return remote(act_hbm, ref, s1_send.at[0], s1_recv.at[0], on_chip)

    def s2(h):
        ref = acts_away.at[own_tiles(core, *act_cuts[h])]
        return remote(act_hbm.at[pl.ds(*act_cuts[h])], ref, s2_send.at[h], s2_recv.at[h], across)

    def s3(at_core, h):
        ref = acts_away.at[own_tiles(at_core, *act_cuts[h])]
        return remote(ref, ref, s3_send.at[h], s3_recv.at[h], on_chip)

    def region(kind, of_chip, start, count):
        first = (of_chip * early, (1 - of_chip) * early, 2 * early)[kind]
        return pl.ds(pl.multiple_of(first + start, TILE), count)

    sizes = (early, early, rest)
    kinds = (0, 1, 2) if rest else (0, 1)

    def t1(f, kind):
        ref = codes.at[f, region(kind, chip, 0, sizes[kind])]
        return remote(ref, ref, t1_send.at[kind], t1_recv.at[kind], on_chip)

    def t2(f, p, of_chip):
        kind, start, count = pieces[p]
        ref = codes.at[f, region(kind, of_chip, start, count)]
        return remote(ref, ref, t2_send.at[p], t2_recv.at[p], across)

    def t3(f, p):
        kind, start, count = pieces[p]
        ref = codes.at[f, region(kind, other, start, count)]
        return remote(ref, ref, t3_send.at[p], t3_recv.at[p], on_chip)

    def send(kind):
        t1(me, kind).start()
        for p, piece in enumerate(pieces):
            if piece[0] == kind:
                t2(me, p, chip).start()

    for h in range(len(act_cuts)):
        s2(h).start()
    s1(core).start()
    load_dec.start()
    load_targets.start()

    def mark(at, live, where):
        keep[at] = (lax.broadcasted_iota(jnp.int32, (TILE, keep.shape[1]), 0) < live).astype(
            jnp.float32
        )
        packed_targets[at] = targets[where]

    def pack(acts, of_chip):
        first_live = live_ref[base + 2 * of_chip]
        second_live = live_ref[base + 2 * of_chip + 1]

        def one(k, carry):
            where, live = tile_of(first_live, second_live, block_tiles, k)
            at = pl.ds(pl.multiple_of(of_chip * early + k * TILE, TILE), TILE)
            packed[at] = acts[where]
            mark(at, live, of_chip * 2 * block_tiles + where)
            return carry

        lax.fori_loop(0, early // TILE, one, 0)

    def pack_rest():
        lives = [live_ref[base + b] for b in range(4)]
        first_extra = jnp.maximum(
            (lives[0] + TILE - 1 >> 4) + (lives[1] + TILE - 1 >> 4) - early // TILE, 0
        )

        def one(k, carry):
            from_first = step(first_extra - k)
            index = early // TILE + k - (1 - from_first) * first_extra
            where0, live0 = tile_of(lives[0], lives[1], block_tiles, index)
            where1, live1 = tile_of(lives[2], lives[3], block_tiles, index)
            where_home = where0 + chip * (where1 - where0)
            where_away = where1 + chip * (where0 - where1)
            at = pl.ds(pl.multiple_of(2 * early + k * TILE, TILE), TILE)
            mine = jnp.full((TILE, acts_home.shape[2]), from_first + chip, jnp.int32) == 1
            packed[at] = jnp.where(mine, acts_home[where_home], acts_away[where_away])
            mark(
                at,
                live1 + from_first * (live0 - live1),
                where1 + 2 * block_tiles + from_first * (where0 - where1 - 2 * block_tiles),
            )
            return carry

        lax.fori_loop(0, rest // TILE, one, 0)

    def encode(kind):
        here = region(kind, chip, 0, sizes[kind])

        def column(n, carry):
            at = pl.ds(pl.multiple_of(n * column_tile, column_tile), column_tile)
            product = jnp.dot(packed[here], enc[:, at], preferred_element_type=jnp.float32)
            value = product.astype(jnp.bfloat16).astype(jnp.float32) + bias_ref[:, at]
            codes[me, here, at] = jnp.maximum(value, 0.0).astype(jnp.bfloat16)
            return carry

        lax.fori_loop(0, columns, column, 0)

    def home_features(kind):
        here = region(kind, chip, 0, sizes[kind])

        def column(n, carry):
            at = pl.ds(pl.multiple_of(n * column_tile, column_tile), column_tile)
            first = jnp.dot(
                codes[me, here], dec[me, :, at], preferred_element_type=jnp.float32
            )
            second = jnp.dot(
                codes[twin, here], dec[twin, :, at], preferred_element_type=jnp.float32
            )
            part[here, at] = first + second
            return carry

        lax.fori_loop(0, columns, column, 0)

    def finish(p):
        kind, start, count = pieces[p]
        here = region(kind, other, start, count)
        step = column_tile if count > 64 else width

        def add(f):
            def column(n, carry):
                at = pl.ds(pl.multiple_of(n * step, step), step)
                part[here, at] += jnp.dot(
                    codes[f, here], dec[f, :, at], preferred_element_type=jnp.float32
                )
                return carry

            lax.fori_loop(0, width // step, column, 0)

        t2(peer, p, other).wait_recv()
        t3(peer, p).start()
        add(peer)
        t3(peer_twin, p).wait_recv()
        add(peer_twin)
        whole = part[here].astype(jnp.bfloat16)
        summed[here] = whole
        error = (
            whole.astype(jnp.float32)
            + dec_bias_ref[...]
            - packed_targets[here].astype(jnp.float32)
        )
        live = jnp.concatenate([keep[here]] * (width // keep.shape[1]), axis=1)
        residual[here] = jnp.where(live > 0.0, error, 0.0).astype(jnp.bfloat16)

    load_live.wait()
    load_bias.wait()
    load_dec_bias.wait()
    load_act.wait()
    s1(1 - core).wait_recv()
    load_targets.wait()
    pack(acts_home, chip)
    load_enc.wait()
    encode(0)
    send(0)
    load_dec.wait()
    t1(twin, 0).wait_recv()
    home_features(0)

    for h in range(len(act_cuts)):
        s2(h).wait_recv()
        s3(core, h).start()
    for h in range(len(act_cuts)):
        s3(1 - core, h).wait_recv()
    pack(acts_away, other)
    encode(1)
    send(1)
    if rest:
        pack_rest()
        encode(2)
        send(2)
    for kind in kinds[1:]:
        t1(twin, kind).wait_recv()
        home_features(kind)
    for p in range(len(pieces)):
        finish(p)

    s1(core).wait_send()
    for h in range(len(act_cuts)):
        s2(h).wait_send()
        s3(core, h).wait_send()
    for kind in kinds:
        t1(me, kind).wait_send()
    for p in range(len(pieces)):
        t2(me, p, chip).wait_send()
        t3(peer, p).wait_send()


def gradient_kernel(
    span,
    early,
    live_ref,
    codes_ref,
    residual_ref,
    summed_ref,
    bias_ref,
    rebuilt_hbm,
    grad_hbm,
    grad,
    rebuilt,
    sem,
):
    owners, width = codes_ref.shape[0], codes_ref.shape[2]
    block_tiles = rebuilt.shape[0] // TILE // 4
    base = lax.axis_index("blk") // 4 * 4
    per = width // span

    def out(f, i):
        at = pl.ds(pl.multiple_of(i * span, span), span)
        return pltpu.make_async_copy(grad.at[f, at], grad_hbm.at[f, at], sem.at[f * per + i])

    def block(f, i):
        at = pl.ds(i * span, span)
        grad[f, at] = lax.dot_general(
            codes_ref[f, :, at],
            residual_ref[...],
            (((0,), (0,)), ((), ())),
            preferred_element_type=jnp.float32,
        )
        out(f, i).start()

    lives = [live_ref[base + b] for b in range(4)]
    counts = [live + TILE - 1 >> 4 for live in lives]
    first_extra = jnp.maximum(counts[0] + counts[1] - early // TILE, 0)

    def spread(b):
        chip = b // 2
        before = counts[b - 1] if b % 2 else 0

        def one(s, carry):
            k = before + s
            place = jnp.where(
                k < early // TILE,
                chip * (early // TILE) + k,
                early // TILE + chip * first_extra + k,
            )
            place = jnp.where(s < counts[b], place, 0)
            value = summed_ref[pl.ds(pl.multiple_of(place * TILE, TILE), TILE)].astype(jnp.float32)
            row = TILE * s + lax.broadcasted_iota(jnp.int32, value.shape, 0)
            at = pl.ds(pl.multiple_of((b * block_tiles + s) * TILE, TILE), TILE)
            rebuilt[at] = jnp.where(row < lives[b], value, 0.0) + bias_ref[...]
            return carry

        lax.fori_loop(0, block_tiles, one, 0)

    def owner(f, carry):
        for i in range(per):
            block(f, i)
        return carry

    lax.fori_loop(0, owners // 2, owner, 0)
    for b in range(4):
        spread(b)
    give = pltpu.make_async_copy(rebuilt, rebuilt_hbm, sem.at[owners * per])
    give.start()
    lax.fori_loop(owners // 2, owners, owner, 0)

    def ended(i, carry):
        out(i // per, i % per).wait()
        return carry

    lax.fori_loop(0, owners * per, ended, 0)
    give.wait()


def packed_tiles(
    order,
    tiles,
    activations,
    live_rows,
    encoder_weight,
    encoder_bias,
    decoder_weight,
    decoder_bias,
    targets,
):
    rows, depth = activations.shape
    features = encoder_weight.shape[1]
    width = decoder_weight.shape[2]
    tokens = targets.shape[0]
    total = TILE * tiles
    early = total - 2 * rows
    block_tiles = rows // TILE
    half = (block_tiles + 1) // 2
    act_cuts = [(0, half), (half, block_tiles - half)]
    act_cuts = [cut for cut in act_cuts if cut[1]]
    pieces = pieces_of(early, total - 2 * early)
    lanes = min(128, width)
    any_space = pl.BlockSpec(memory_space=pl.ANY)
    stay = functools.partial(pltpu.with_memory_space_constraint, memory_space=pltpu.HBM)
    in_vmem = pl.BlockSpec(memory_space=pltpu.VMEM)
    in_smem = pl.BlockSpec(memory_space=pltpu.SMEM)
    in_hbm = pl.BlockSpec(memory_space=pltpu.HBM)
    dma = pltpu.SemaphoreType.DMA
    bf16 = jnp.bfloat16
    f32 = jnp.float32
    codes, residual, summed = pl.pallas_call(
        functools.partial(gather_kernel, act_cuts, early, pieces),
        out_shape=(
            pltpu.VMEM((4, total, features), bf16),
            pltpu.VMEM((total, width), bf16),
            pltpu.VMEM((total, width), bf16),
        ),
        in_specs=[in_hbm] * 7,
        out_specs=(in_vmem, in_vmem, in_vmem),
        scratch_shapes=[
            pltpu.VMEM((2 * block_tiles, TILE, depth), bf16),
            pltpu.VMEM((2 * block_tiles, TILE, depth), bf16),
            pltpu.VMEM((total, depth), bf16),
            pltpu.VMEM((depth, features), bf16),
            pltpu.VMEM((4, features, width), bf16),
            pltpu.VMEM((total, width), f32),
            pltpu.VMEM((4 * block_tiles, TILE, width), bf16),
            pltpu.VMEM((total, width), bf16),
            pltpu.VMEM((total, lanes), f32),
            pltpu.SMEM(live_rows.shape, jnp.int32),
            pltpu.VMEM((1, features), f32),
            pltpu.VMEM((1, width), f32),
            dma((7,)),
            dma((1,)),
            dma((1,)),
            dma((len(act_cuts),)),
            dma((len(act_cuts),)),
            dma((len(act_cuts),)),
            dma((len(act_cuts),)),
            dma((3,)),
            dma((3,)),
            dma((len(pieces),)),
            dma((len(pieces),)),
            dma((len(pieces),)),
            dma((len(pieces),)),
        ],
        compiler_params=pltpu.CompilerParams(
            collective_id=order, has_side_effects=True, vmem_limit_bytes=44 * 1024 * 1024
        ),
        name=f"gather_codes_{tiles}",
    )(
        activations.reshape(block_tiles, TILE, depth),
        stay(live_rows),
        encoder_weight,
        stay(encoder_bias[None, :]),
        decoder_weight,
        stay(decoder_bias[None, :]),
        targets.reshape(4 * block_tiles, TILE, width),
    )

    span = min(256, features)
    rebuilt, grad = pl.pallas_call(
        functools.partial(gradient_kernel, span, early),
        out_shape=(
            jax.ShapeDtypeStruct((tokens, width), f32),
            jax.ShapeDtypeStruct((4, features, width), f32),
        ),
        in_specs=[in_smem, in_vmem, in_vmem, in_vmem, in_vmem],
        out_specs=(any_space, any_space),
        scratch_shapes=[
            pltpu.VMEM((4, features, width), f32),
            pltpu.VMEM((tokens, width), f32),
            dma((4 * (features // span) + 1,)),
        ],
        compiler_params=pltpu.CompilerParams(vmem_limit_bytes=44 * 1024 * 1024),
        name=f"gradient_{tiles}",
    )(live_rows, codes, residual, summed, decoder_bias[None, :])
    return rebuilt, grad


def four_owners(activations, live_rows, *operands):
    rows = activations.shape[0]
    if rows % TILE:
        return general(activations, live_rows, *operands)
    block_tiles = rows // TILE
    sizes = sorted({2 * block_tiles + max(1, block_tiles * k // 10) for k in (9, 12, 15, 20)})
    most = (live_rows + TILE - 1 >> 4).reshape(-1, 4).sum(1).max()
    choice = sum((most > size).astype(jnp.int32) for size in sizes[:-1])
    return lax.switch(
        choice,
        [functools.partial(packed_tiles, order, tiles) for order, tiles in enumerate(sizes)],
        activations,
        live_rows,
        *operands,
    )


def from_partner(shard, axis, distance):
    return lax.ppermute(shard, axis, [(i, i ^ 1 << distance) for i in range(lax.axis_size(axis))])


def group_rows(block, levels, position):
    for bit in range(levels):
        other = from_partner(block, "blk", bit)
        upper = position >> bit & 1 == 1
        block = jnp.where(
            upper, jnp.concatenate([other, block], 0), jnp.concatenate([block, other], 0)
        )
    return block


def general(
    activations, live_rows, encoder_weight, encoder_bias, decoder_weight, decoder_bias, targets
):
    owners = lax.axis_size("blk") // G
    levels = owners.bit_length() - 1
    shares = lax.axis_size("feat")
    position = lax.axis_index("blk")
    share_index = lax.axis_index("feat")
    group_index = position // owners
    tok_rows = activations.shape[0]
    counts = lax.dynamic_slice_in_dim(live_rows, group_index * owners, owners)
    positions = jnp.arange(tok_rows, dtype=jnp.int32)
    live_mask = (positions[None, :] < counts[:, None]).astype(jnp.float32).reshape(-1)
    gathered = group_rows(activations, levels, position)
    per_share = encoder_weight.shape[1] // shares
    bias_share = lax.dynamic_slice_in_dim(encoder_bias, share_index * per_share, per_share)
    columns = encoder_weight
    whole = lax.psum(
        lax.dot_general(
            columns, gathered, (((0,), (1,)), ((), ())), preferred_element_type=jnp.float32
        ).astype(jnp.bfloat16),
        "feat",
    ).astype(jnp.float32)
    preact = lax.dynamic_slice_in_dim(whole, share_index * per_share, per_share, 0)
    codes_by_feature = (jax.nn.relu(preact + bias_share[:, None]) * live_mask[None, :]).astype(
        jnp.bfloat16
    )
    codes_all = group_rows(codes_by_feature, levels, position)
    decoder_rows = decoder_weight.reshape(-1, decoder_weight.shape[2])
    block_rows = gathered.shape[0] // shares
    columns = codes_all
    summed = lax.psum_scatter(
        lax.dot_general(
            columns, decoder_rows, (((0,), (0,)), ((), ())), preferred_element_type=jnp.float32
        ).astype(jnp.bfloat16),
        "feat",
        scatter_dimension=0,
        tiled=True,
    ).astype(jnp.float32)
    rebuilt = summed + decoder_bias[None, :]
    mask_block = lax.dynamic_slice_in_dim(live_mask, share_index * block_rows, block_rows)
    residual = ((rebuilt - targets.astype(jnp.float32)) * mask_block[:, None]).astype(jnp.bfloat16)
    columns = codes_all
    gradient = jnp.dot(
        columns,
        lax.all_gather(residual, "feat", axis=0, tiled=True),
        preferred_element_type=jnp.float32,
    )
    return (rebuilt, gradient.reshape(decoder_weight.shape))


def solution(mesh):
    in_specs = (
        P("blk", "feat"),
        P(),
        P("feat", "blk"),
        P("blk"),
        P(None, "feat", "blk"),
        P("blk"),
        P("feat", "blk"),
    )
    out_specs = (P("feat", "blk"), P(None, "feat", "blk"))
    fused = mesh.shape["blk"] // G == 4 and mesh.shape["feat"] == 1
    return jax.shard_map(
        four_owners if fused else general,
        mesh=mesh,
        in_specs=in_specs,
        out_specs=out_specs,
        check_vma=False,
    )
```

```python
import functools

import jax
import jax.numpy as jnp
from jax import lax
from jax.experimental import pallas as pl
from jax.experimental.pallas import tpu as pltpu
from jax.sharding import PartitionSpec as P

G = 8
TILE = 16
MESH = pl.DeviceIdType.MESH


def cuts(rows, parts):
    if rows % 16 or rows // 16 < len(parts):
        return [(0, rows)]
    tiles, total, edges = rows // 16, sum(parts), [0]
    for k in range(1, len(parts)):
        edges.append(max(edges[-1] + 1, tiles * sum(parts[:k]) // total))
    edges.append(tiles)
    return [(16 * a, 16 * (b - a)) for a, b in zip(edges[:-1], edges[1:])]


def pieces_of(early, rest):
    first = [(0, *cut) for cut in cuts(early, (1,))]
    if rest:
        late = [(1, *cut) for cut in cuts(early, (1,))]
        return first + late + [(2, *cut) for cut in cuts(rest, (1,))]
    return first + [(1, *cut) for cut in cuts(early, (1, 1))]


def step(count):
    return jnp.clip(count, 0, 1)


def tile_of(first_live, second_live, tiles, k):
    first = first_live + TILE - 1 >> 4
    second = second_live + TILE - 1 >> 4
    late = 1 - step(first - k)
    inside = jnp.minimum(k - late * first, tiles - 1)
    live = first_live + late * (second_live - first_live) - TILE * inside
    return inside + late * tiles, step(first + second - k) * live


def gather_kernel(
    act_cuts,
    early,
    pieces,
    act_hbm,
    live_hbm,
    enc_hbm,
    bias_hbm,
    dec_hbm,
    dec_bias_hbm,
    targets_hbm,
    codes,
    residual,
    summed,
    acts_home,
    acts_away,
    packed,
    enc,
    dec,
    part,
    targets,
    packed_targets,
    keep,
    live_ref,
    bias_ref,
    dec_bias_ref,
    load_sem,
    s1_send,
    s1_recv,
    s2_send,
    s2_recv,
    s3_send,
    s3_recv,
    t1_send,
    t1_recv,
    t2_send,
    t2_recv,
    t3_send,
    t3_recv,
):
    position = lax.axis_index("blk")
    share = lax.axis_index("feat")
    base = position // 4 * 4
    me = position % 4
    core = me % 2
    home = me - core
    away = 2 - home
    chip = home // 2
    other = 1 - chip
    twin = home + 1 - core
    peer = away + core
    peer_twin = away + 1 - core
    on_chip = (base + twin, share)
    across = (base + peer, share)

    block_tiles = act_hbm.shape[0]
    total = codes.shape[1]
    rest = total - 2 * early
    width = enc.shape[1]
    column_tile = min(256, width)
    columns = width // column_tile

    def own_tiles(at_core, start, count):
        return pl.ds(at_core * block_tiles + start, count)

    load_act = pltpu.make_async_copy(
        act_hbm, acts_home.at[own_tiles(core, 0, block_tiles)], load_sem.at[0]
    )
    load_enc = pltpu.make_async_copy(enc_hbm, enc, load_sem.at[1])
    load_dec = pltpu.make_async_copy(dec_hbm, dec, load_sem.at[2])
    load_targets = pltpu.make_async_copy(targets_hbm, targets, load_sem.at[3])
    load_live = pltpu.make_async_copy(live_hbm, live_ref, load_sem.at[4])
    load_bias = pltpu.make_async_copy(bias_hbm, bias_ref, load_sem.at[5])
    load_dec_bias = pltpu.make_async_copy(dec_bias_hbm, dec_bias_ref, load_sem.at[6])
    load_live.start()
    load_bias.start()
    load_act.start()
    load_enc.start()
    load_dec_bias.start()

    barrier = pltpu.get_barrier_semaphore()
    for neighbour in (on_chip, across):
        pl.semaphore_signal(barrier, inc=1, device_id=neighbour, device_id_type=MESH)
    pl.semaphore_wait(barrier, 2)

    def remote(src, dst, send, recv, to):
        return pltpu.make_async_remote_copy(
            src_ref=src,
            dst_ref=dst,
            send_sem=send,
            recv_sem=recv,
            device_id=to,
            device_id_type=MESH,
        )

    def s1(at_core):
        ref = acts_home.at[own_tiles(at_core, 0, block_tiles)]
        return remote(act_hbm, ref, s1_send.at[0], s1_recv.at[0], on_chip)

    def s2(h):
        ref = acts_away.at[own_tiles(core, *act_cuts[h])]
        return remote(act_hbm.at[pl.ds(*act_cuts[h])], ref, s2_send.at[h], s2_recv.at[h], across)

    def s3(at_core, h):
        ref = acts_away.at[own_tiles(at_core, *act_cuts[h])]
        return remote(ref, ref, s3_send.at[h], s3_recv.at[h], on_chip)

    def region(kind, of_chip, start, count):
        first = (of_chip * early, (1 - of_chip) * early, 2 * early)[kind]
        return pl.ds(pl.multiple_of(first + start, TILE), count)

    sizes = (early, early, rest)
    kinds = (0, 1, 2) if rest else (0, 1)

    def t1(f, kind):
        ref = codes.at[f, region(kind, chip, 0, sizes[kind])]
        return remote(ref, ref, t1_send.at[kind], t1_recv.at[kind], on_chip)

    def t2(f, p, of_chip):
        kind, start, count = pieces[p]
        ref = codes.at[f, region(kind, of_chip, start, count)]
        return remote(ref, ref, t2_send.at[p], t2_recv.at[p], across)

    def t3(f, p):
        kind, start, count = pieces[p]
        ref = codes.at[f, region(kind, other, start, count)]
        return remote(ref, ref, t3_send.at[p], t3_recv.at[p], on_chip)

    def send(kind):
        t1(me, kind).start()
        for p, piece in enumerate(pieces):
            if piece[0] == kind:
                t2(me, p, chip).start()

    for h in range(len(act_cuts)):
        s2(h).start()
    s1(core).start()
    load_dec.start()
    load_targets.start()

    def mark(at, live, where):
        keep[at] = (lax.broadcasted_iota(jnp.int32, (TILE, keep.shape[1]), 0) < live).astype(
            jnp.float32
        )
        packed_targets[at] = targets[where]

    def pack(acts, of_chip):
        first_live = live_ref[base + 2 * of_chip]
        second_live = live_ref[base + 2 * of_chip + 1]

        def one(k, carry):
            where, live = tile_of(first_live, second_live, block_tiles, k)
            at = pl.ds(pl.multiple_of(of_chip * early + k * TILE, TILE), TILE)
            packed[at] = acts[where]
            mark(at, live, of_chip * 2 * block_tiles + where)
            return carry

        lax.fori_loop(0, early // TILE, one, 0)

    def pack_rest():
        lives = [live_ref[base + b] for b in range(4)]
        first_extra = jnp.maximum(
            (lives[0] + TILE - 1 >> 4) + (lives[1] + TILE - 1 >> 4) - early // TILE, 0
        )

        def one(k, carry):
            from_first = step(first_extra - k)
            index = early // TILE + k - (1 - from_first) * first_extra
            where0, live0 = tile_of(lives[0], lives[1], block_tiles, index)
            where1, live1 = tile_of(lives[2], lives[3], block_tiles, index)
            where_home = where0 + chip * (where1 - where0)
            where_away = where1 + chip * (where0 - where1)
            at = pl.ds(pl.multiple_of(2 * early + k * TILE, TILE), TILE)
            mine = jnp.full((TILE, acts_home.shape[2]), from_first + chip, jnp.int32) == 1
            packed[at] = jnp.where(mine, acts_home[where_home], acts_away[where_away])
            mark(
                at,
                live1 + from_first * (live0 - live1),
                where1 + 2 * block_tiles + from_first * (where0 - where1 - 2 * block_tiles),
            )
            return carry

        lax.fori_loop(0, rest // TILE, one, 0)

    def encode(kind):
        here = region(kind, chip, 0, sizes[kind])

        def column(n, carry):
            at = pl.ds(pl.multiple_of(n * column_tile, column_tile), column_tile)
            product = jnp.dot(packed[here], enc[:, at], preferred_element_type=jnp.float32)
            value = product.astype(jnp.bfloat16).astype(jnp.float32) + bias_ref[:, at]
            codes[me, here, at] = jnp.maximum(value, 0.0).astype(jnp.bfloat16)
            return carry

        lax.fori_loop(0, columns, column, 0)

    def home_features(kind):
        here = region(kind, chip, 0, sizes[kind])

        def column(n, carry):
            at = pl.ds(pl.multiple_of(n * column_tile, column_tile), column_tile)
            first = jnp.dot(
                codes[me, here], dec[me, :, at], preferred_element_type=jnp.float32
            )
            second = jnp.dot(
                codes[twin, here], dec[twin, :, at], preferred_element_type=jnp.float32
            )
            part[here, at] = first + second
            return carry

        lax.fori_loop(0, columns, column, 0)

    def finish(p):
        kind, start, count = pieces[p]
        here = region(kind, other, start, count)

        def add(owners, span):
            def column(n, carry):
                at = pl.ds(pl.multiple_of(n * span, span), span)
                total = part[here, at]
                for f in owners:
                    total += jnp.dot(
                        codes[f, here], dec[f, :, at], preferred_element_type=jnp.float32
                    )
                part[here, at] = total
                return carry

            lax.fori_loop(0, width // span, column, 0)

        t2(peer, p, other).wait_recv()
        t3(peer, p).start()
        if p == len(pieces) - 1:
            add([peer], width)
            t3(peer_twin, p).wait_recv()
            add([peer_twin], width)
        else:
            t3(peer_twin, p).wait_recv()
            add([peer, peer_twin], column_tile)
        whole = part[here].astype(jnp.bfloat16)
        summed[here] = whole
        error = (
            whole.astype(jnp.float32)
            + dec_bias_ref[...]
            - packed_targets[here].astype(jnp.float32)
        )
        live = jnp.concatenate([keep[here]] * (width // keep.shape[1]), axis=1)
        residual[here] = jnp.where(live > 0.0, error, 0.0).astype(jnp.bfloat16)

    load_live.wait()
    load_bias.wait()
    load_dec_bias.wait()
    load_act.wait()
    s1(1 - core).wait_recv()
    load_targets.wait()
    pack(acts_home, chip)
    load_enc.wait()
    encode(0)
    send(0)
    load_dec.wait()
    t1(twin, 0).wait_recv()
    home_features(0)

    for h in range(len(act_cuts)):
        s2(h).wait_recv()
        s3(core, h).start()
    for h in range(len(act_cuts)):
        s3(1 - core, h).wait_recv()
    pack(acts_away, other)
    encode(1)
    send(1)
    if rest:
        pack_rest()
        encode(2)
        send(2)
    for kind in kinds[1:]:
        t1(twin, kind).wait_recv()
        home_features(kind)
    for p in range(len(pieces)):
        finish(p)

    s1(core).wait_send()
    for h in range(len(act_cuts)):
        s2(h).wait_send()
        s3(core, h).wait_send()
    for kind in kinds:
        t1(me, kind).wait_send()
    for p in range(len(pieces)):
        t2(me, p, chip).wait_send()
        t3(peer, p).wait_send()


def choice_kernel(sizes, live_ref, choice_ref):
    most = 0
    for group in range(0, live_ref.shape[0], 4):
        most = jnp.maximum(most, sum(live_ref[group + b] + TILE - 1 >> 4 for b in range(4)))
    choice_ref[0] = sum((most > size).astype(jnp.int32) for size in sizes[:-1])


def gradient_kernel(
    span,
    early,
    live_ref,
    codes_ref,
    residual_ref,
    summed_ref,
    bias_ref,
    rebuilt_hbm,
    grad_hbm,
    grad,
    rebuilt,
    sem,
):
    owners, width = codes_ref.shape[0], codes_ref.shape[2]
    block_tiles = rebuilt.shape[0] // TILE // 4
    base = lax.axis_index("blk") // 4 * 4
    per = width // span

    def out(f, i):
        at = pl.ds(pl.multiple_of(i * span, span), span)
        return pltpu.make_async_copy(grad.at[f, at], grad_hbm.at[f, at], sem.at[f * per + i])

    def block(f, i):
        at = pl.ds(i * span, span)
        grad[f, at] = lax.dot_general(
            codes_ref[f, :, at],
            residual_ref[...],
            (((0,), (0,)), ((), ())),
            preferred_element_type=jnp.float32,
        )
        out(f, i).start()

    counts = [live_ref[base + b] + TILE - 1 >> 4 for b in range(4)]
    first_extra = jnp.maximum(counts[0] + counts[1] - early // TILE, 0)

    def spread(b, s):
        live = live_ref[base + b]
        chip = b // 2
        k = b % 2 * (live_ref[base + b - b % 2] + TILE - 1 >> 4) + s
        place = jnp.where(
            k < early // TILE,
            chip * (early // TILE) + k,
            early // TILE + chip * first_extra + k,
        )
        place = jnp.where(TILE * s < live, place, 0)
        value = summed_ref[pl.ds(pl.multiple_of(place * TILE, TILE), TILE)].astype(jnp.float32)
        row = TILE * s + lax.broadcasted_iota(jnp.int32, value.shape, 0)
        at = pl.ds(pl.multiple_of((b * block_tiles + s) * TILE, TILE), TILE)
        rebuilt[at] = jnp.where(row < live, value, 0.0) + bias_ref[...]

    def give(b):
        at = pl.ds(pl.multiple_of(b * block_tiles * TILE, TILE), block_tiles * TILE)
        return pltpu.make_async_copy(rebuilt.at[at], rebuilt_hbm.at[at], sem.at[owners * per + b])

    def owner(f, carry):
        for i in range(per):
            block(f, i)
            for s in range(block_tiles * i // per, block_tiles * (i + 1) // per):
                spread(f, s)
        give(f).start()
        return carry

    lax.fori_loop(0, 4, owner, 0)

    def ended(i, carry):
        out(i // per, i % per).wait()
        return carry

    lax.fori_loop(0, owners * per, ended, 0)
    for b in range(4):
        give(b).wait()


def packed_tiles(
    order,
    tiles,
    activations,
    live_rows,
    encoder_weight,
    encoder_bias,
    decoder_weight,
    decoder_bias,
    targets,
):
    rows, depth = activations.shape
    features = encoder_weight.shape[1]
    width = decoder_weight.shape[2]
    tokens = targets.shape[0]
    total = TILE * tiles
    early = total - 2 * rows
    block_tiles = rows // TILE
    half = (block_tiles + 1) // 2
    act_cuts = [(0, block_tiles)]
    act_cuts = [cut for cut in act_cuts if cut[1]]
    pieces = pieces_of(early, total - 2 * early)
    lanes = min(128, width)
    any_space = pl.BlockSpec(memory_space=pl.ANY)
    stay = functools.partial(pltpu.with_memory_space_constraint, memory_space=pltpu.HBM)
    in_vmem = pl.BlockSpec(memory_space=pltpu.VMEM)
    in_smem = pl.BlockSpec(memory_space=pltpu.SMEM)
    in_hbm = pl.BlockSpec(memory_space=pltpu.HBM)
    dma = pltpu.SemaphoreType.DMA
    bf16 = jnp.bfloat16
    f32 = jnp.float32
    codes, residual, summed = pl.pallas_call(
        functools.partial(gather_kernel, act_cuts, early, pieces),
        out_shape=(
            pltpu.VMEM((4, total, features), bf16),
            pltpu.VMEM((total, width), bf16),
            pltpu.VMEM((total, width), bf16),
        ),
        in_specs=[in_hbm] * 7,
        out_specs=(in_vmem, in_vmem, in_vmem),
        scratch_shapes=[
            pltpu.VMEM((2 * block_tiles, TILE, depth), bf16),
            pltpu.VMEM((2 * block_tiles, TILE, depth), bf16),
            pltpu.VMEM((total, depth), bf16),
            pltpu.VMEM((depth, features), bf16),
            pltpu.VMEM((4, features, width), bf16),
            pltpu.VMEM((total, width), f32),
            pltpu.VMEM((4 * block_tiles, TILE, width), bf16),
            pltpu.VMEM((total, width), bf16),
            pltpu.VMEM((total, lanes), f32),
            pltpu.SMEM(live_rows.shape, jnp.int32),
            pltpu.VMEM((1, features), f32),
            pltpu.VMEM((1, width), f32),
            dma((7,)),
            dma((1,)),
            dma((1,)),
            dma((len(act_cuts),)),
            dma((len(act_cuts),)),
            dma((len(act_cuts),)),
            dma((len(act_cuts),)),
            dma((3,)),
            dma((3,)),
            dma((len(pieces),)),
            dma((len(pieces),)),
            dma((len(pieces),)),
            dma((len(pieces),)),
        ],
        compiler_params=pltpu.CompilerParams(
            collective_id=order, has_side_effects=True, vmem_limit_bytes=44 * 1024 * 1024
        ),
        name=f"gather_codes_{tiles}",
    )(
        activations.reshape(block_tiles, TILE, depth),
        stay(live_rows),
        encoder_weight,
        stay(encoder_bias[None, :]),
        decoder_weight,
        stay(decoder_bias[None, :]),
        targets.reshape(4 * block_tiles, TILE, width),
    )

    span = min(256, features)
    rebuilt, grad = pl.pallas_call(
        functools.partial(gradient_kernel, span, early),
        out_shape=(
            jax.ShapeDtypeStruct((tokens, width), f32),
            jax.ShapeDtypeStruct((4, features, width), f32),
        ),
        in_specs=[in_smem, in_vmem, in_vmem, in_vmem, in_vmem],
        out_specs=(any_space, any_space),
        scratch_shapes=[
            pltpu.VMEM((4, features, width), f32),
            pltpu.VMEM((tokens, width), f32),
            dma((4 * (features // span) + 4,)),
        ],
        compiler_params=pltpu.CompilerParams(vmem_limit_bytes=44 * 1024 * 1024),
        name=f"gradient_{tiles}",
    )(live_rows, codes, residual, summed, decoder_bias[None, :])
    return rebuilt, grad


def four_owners(activations, live_rows, *operands):
    rows = activations.shape[0]
    if rows % TILE:
        return general(activations, live_rows, *operands)
    block_tiles = rows // TILE
    sizes = sorted({2 * block_tiles + max(1, block_tiles * k // 10) for k in (9, 12, 15, 20)})
    in_smem = pl.BlockSpec(memory_space=pltpu.SMEM)
    choice = pl.pallas_call(
        functools.partial(choice_kernel, sizes),
        out_shape=jax.ShapeDtypeStruct((1,), jnp.int32),
        in_specs=[in_smem],
        out_specs=in_smem,
        name="choice",
    )(live_rows)
    return lax.switch(
        choice[0],
        [functools.partial(packed_tiles, order, tiles) for order, tiles in enumerate(sizes)],
        activations,
        live_rows,
        *operands,
    )


def from_partner(shard, axis, distance):
    return lax.ppermute(shard, axis, [(i, i ^ 1 << distance) for i in range(lax.axis_size(axis))])


def group_rows(block, levels, position):
    for bit in range(levels):
        other = from_partner(block, "blk", bit)
        upper = position >> bit & 1 == 1
        block = jnp.where(
            upper, jnp.concatenate([other, block], 0), jnp.concatenate([block, other], 0)
        )
    return block


def general(
    activations, live_rows, encoder_weight, encoder_bias, decoder_weight, decoder_bias, targets
):
    owners = lax.axis_size("blk") // G
    levels = owners.bit_length() - 1
    shares = lax.axis_size("feat")
    position = lax.axis_index("blk")
    share_index = lax.axis_index("feat")
    group_index = position // owners
    tok_rows = activations.shape[0]
    counts = lax.dynamic_slice_in_dim(live_rows, group_index * owners, owners)
    positions = jnp.arange(tok_rows, dtype=jnp.int32)
    live_mask = (positions[None, :] < counts[:, None]).astype(jnp.float32).reshape(-1)
    gathered = group_rows(activations, levels, position)
    per_share = encoder_weight.shape[1] // shares
    bias_share = lax.dynamic_slice_in_dim(encoder_bias, share_index * per_share, per_share)
    columns = encoder_weight
    whole = lax.psum(
        lax.dot_general(
            columns, gathered, (((0,), (1,)), ((), ())), preferred_element_type=jnp.float32
        ).astype(jnp.bfloat16),
        "feat",
    ).astype(jnp.float32)
    preact = lax.dynamic_slice_in_dim(whole, share_index * per_share, per_share, 0)
    codes_by_feature = (jax.nn.relu(preact + bias_share[:, None]) * live_mask[None, :]).astype(
        jnp.bfloat16
    )
    codes_all = group_rows(codes_by_feature, levels, position)
    decoder_rows = decoder_weight.reshape(-1, decoder_weight.shape[2])
    block_rows = gathered.shape[0] // shares
    columns = codes_all
    summed = lax.psum_scatter(
        lax.dot_general(
            columns, decoder_rows, (((0,), (0,)), ((), ())), preferred_element_type=jnp.float32
        ).astype(jnp.bfloat16),
        "feat",
        scatter_dimension=0,
        tiled=True,
    ).astype(jnp.float32)
    rebuilt = summed + decoder_bias[None, :]
    mask_block = lax.dynamic_slice_in_dim(live_mask, share_index * block_rows, block_rows)
    residual = ((rebuilt - targets.astype(jnp.float32)) * mask_block[:, None]).astype(jnp.bfloat16)
    columns = codes_all
    gradient = jnp.dot(
        columns,
        lax.all_gather(residual, "feat", axis=0, tiled=True),
        preferred_element_type=jnp.float32,
    )
    return (rebuilt, gradient.reshape(decoder_weight.shape))


def solution(mesh):
    in_specs = (
        P("blk", "feat"),
        P(),
        P("feat", "blk"),
        P("blk"),
        P(None, "feat", "blk"),
        P("blk"),
        P("feat", "blk"),
    )
    out_specs = (P("feat", "blk"), P(None, "feat", "blk"))
    fused = mesh.shape["blk"] // G == 4 and mesh.shape["feat"] == 1
    return jax.shard_map(
        four_owners if fused else general,
        mesh=mesh,
        in_specs=in_specs,
        out_specs=out_specs,
        check_vma=False,
    )
```

```python
import functools

import jax
import jax.numpy as jnp
from jax import lax
from jax.experimental import pallas as pl
from jax.experimental.pallas import tpu as pltpu
from jax.sharding import PartitionSpec as P

G = 8
TILE = 16
MESH = pl.DeviceIdType.MESH


def cuts(rows, parts):
    if rows % 16 or rows // 16 < len(parts):
        return [(0, rows)]
    tiles, total, edges = rows // 16, sum(parts), [0]
    for k in range(1, len(parts)):
        edges.append(max(edges[-1] + 1, tiles * sum(parts[:k]) // total))
    edges.append(tiles)
    return [(16 * a, 16 * (b - a)) for a, b in zip(edges[:-1], edges[1:])]


def pieces_of(early, rest):
    first = [(0, *cut) for cut in cuts(early, (1,))]
    if rest:
        late = [(1, *cut) for cut in cuts(early, (1,))]
        return first + late + [(2, *cut) for cut in cuts(rest, (1,))]
    return first + [(1, *cut) for cut in cuts(early, (1, 1))]


def step(count):
    return jnp.clip(count, 0, 1)


def tile_of(first_live, second_live, tiles, k):
    first = first_live + TILE - 1 >> 4
    second = second_live + TILE - 1 >> 4
    late = 1 - step(first - k)
    inside = jnp.minimum(k - late * first, tiles - 1)
    live = first_live + late * (second_live - first_live) - TILE * inside
    return late, inside, step(first + second - k) * live


def slot_of(late, inside, sent):
    over = step(inside - sent + 1)
    return (late + over - 2 * late * over) * sent + inside + over * (2 * sent - 1 - 2 * inside)


def gather_kernel(
    sent,
    early,
    pieces,
    act_hbm,
    live_hbm,
    enc_hbm,
    bias_hbm,
    dec_hbm,
    dec_bias_hbm,
    targets_hbm,
    codes,
    residual,
    summed,
    acts_home,
    acts_away,
    spill,
    packed,
    enc,
    dec,
    part,
    targets,
    packed_targets,
    keep,
    live_ref,
    bias_ref,
    dec_bias_ref,
    load_sem,
    s1_send,
    s1_recv,
    s2_send,
    s2_recv,
    s3_send,
    s3_recv,
    t1_send,
    t1_recv,
    t2_send,
    t2_recv,
    t3_send,
    t3_recv,
):
    position = lax.axis_index("blk")
    share = lax.axis_index("feat")
    base = position // 4 * 4
    me = position % 4
    core = me % 2
    home = me - core
    away = 2 - home
    chip = home // 2
    other = 1 - chip
    twin = home + 1 - core
    peer = away + core
    peer_twin = away + 1 - core
    on_chip = (base + twin, share)
    across = (base + peer, share)

    block_tiles = act_hbm.shape[0]
    spare = block_tiles - sent
    act_cuts = [(0, sent - spare)] + [(sent - spare, spare)] * (spare > 0)
    total = codes.shape[1]
    rest = total - 2 * early
    width = enc.shape[1]
    column_tile = min(256, width)
    columns = width // column_tile

    def own_tiles(at_core, start, count):
        return pl.ds(at_core * block_tiles + start, count)

    load_act = pltpu.make_async_copy(
        act_hbm, acts_home.at[own_tiles(core, 0, block_tiles)], load_sem.at[0]
    )
    load_enc = pltpu.make_async_copy(enc_hbm, enc, load_sem.at[1])
    load_dec = pltpu.make_async_copy(dec_hbm, dec, load_sem.at[2])
    load_targets = pltpu.make_async_copy(targets_hbm, targets, load_sem.at[3])
    load_live = pltpu.make_async_copy(live_hbm, live_ref, load_sem.at[4])
    load_bias = pltpu.make_async_copy(bias_hbm, bias_ref, load_sem.at[5])
    load_dec_bias = pltpu.make_async_copy(dec_bias_hbm, dec_bias_ref, load_sem.at[6])
    load_live.start()
    load_bias.start()
    load_act.start()
    load_enc.start()
    load_dec_bias.start()

    barrier = pltpu.get_barrier_semaphore()
    for neighbour in (on_chip, across):
        pl.semaphore_signal(barrier, inc=1, device_id=neighbour, device_id_type=MESH)
    pl.semaphore_wait(barrier, 2)

    def remote(src, dst, send, recv, to):
        return pltpu.make_async_remote_copy(
            src_ref=src,
            dst_ref=dst,
            send_sem=send,
            recv_sem=recv,
            device_id=to,
            device_id_type=MESH,
        )

    def s1(at_core):
        ref = acts_home.at[own_tiles(at_core, 0, block_tiles)]
        return remote(act_hbm, ref, s1_send.at[0], s1_recv.at[0], on_chip)

    def s2(h):
        at, count = act_cuts[h]
        src = spill if h else act_hbm.at[pl.ds(at, count)]
        ref = acts_away.at[pl.ds(core * sent + at, count)]
        return remote(src, ref, s2_send.at[h], s2_recv.at[h], across)

    def s3(at_core):
        ref = acts_away.at[pl.ds(at_core * sent, sent)]
        return remote(ref, ref, s3_send.at[0], s3_recv.at[0], on_chip)

    def region(kind, of_chip, start, count):
        first = (of_chip * early, (1 - of_chip) * early, 2 * early)[kind]
        return pl.ds(pl.multiple_of(first + start, TILE), count)

    sizes = (early, early, rest)
    kinds = (0, 1, 2) if rest else (0, 1)

    def t1(f, kind):
        ref = codes.at[f, region(kind, chip, 0, sizes[kind])]
        return remote(ref, ref, t1_send.at[kind], t1_recv.at[kind], on_chip)

    def t2(f, p, of_chip):
        kind, start, count = pieces[p]
        ref = codes.at[f, region(kind, of_chip, start, count)]
        return remote(ref, ref, t2_send.at[p], t2_recv.at[p], across)

    def t3(f, p):
        kind, start, count = pieces[p]
        ref = codes.at[f, region(kind, other, start, count)]
        return remote(ref, ref, t3_send.at[p], t3_recv.at[p], on_chip)

    def send(kind):
        t1(me, kind).start()
        for p, piece in enumerate(pieces):
            if piece[0] == kind:
                t2(me, p, chip).start()

    s2(0).start()
    s1(core).start()
    load_dec.start()
    load_targets.start()

    def mark(at, live, where):
        keep[at] = (lax.broadcasted_iota(jnp.int32, (TILE, keep.shape[1]), 0) < live).astype(
            jnp.float32
        )
        packed_targets[at] = targets[where]

    def pack(acts, of_chip):
        first_live = live_ref[base + 2 * of_chip]
        second_live = live_ref[base + 2 * of_chip + 1]

        def one(k, carry):
            late, inside, live = tile_of(first_live, second_live, block_tiles, k)
            where = late * block_tiles + inside
            at = pl.ds(pl.multiple_of(of_chip * early + k * TILE, TILE), TILE)
            packed[at] = acts[slot_of(late, inside, sent) if acts is acts_away else where]
            mark(at, live, of_chip * 2 * block_tiles + where)
            return carry

        lax.fori_loop(0, early // TILE, one, 0)

    def pack_rest():
        lives = [live_ref[base + b] for b in range(4)]
        first_extra = jnp.maximum(
            (lives[0] + TILE - 1 >> 4) + (lives[1] + TILE - 1 >> 4) - early // TILE, 0
        )

        def one(k, carry):
            from_first = step(first_extra - k)
            index = early // TILE + k - (1 - from_first) * first_extra
            late0, inside0, live0 = tile_of(lives[0], lives[1], block_tiles, index)
            late1, inside1, live1 = tile_of(lives[2], lives[3], block_tiles, index)
            where0 = late0 * block_tiles + inside0
            where1 = late1 * block_tiles + inside1
            slot0 = slot_of(late0, inside0, sent)
            slot1 = slot_of(late1, inside1, sent)
            where_home = where0 + chip * (where1 - where0)
            where_away = slot1 + chip * (slot0 - slot1)
            at = pl.ds(pl.multiple_of(2 * early + k * TILE, TILE), TILE)
            mine = jnp.full((TILE, acts_home.shape[2]), from_first + chip, jnp.int32) == 1
            packed[at] = jnp.where(mine, acts_home[where_home], acts_away[where_away])
            mark(
                at,
                live1 + from_first * (live0 - live1),
                where1 + 2 * block_tiles + from_first * (where0 - where1 - 2 * block_tiles),
            )
            return carry

        lax.fori_loop(0, rest // TILE, one, 0)

    def encode(kind):
        here = region(kind, chip, 0, sizes[kind])

        def column(n, carry):
            at = pl.ds(pl.multiple_of(n * column_tile, column_tile), column_tile)
            product = jnp.dot(packed[here], enc[:, at], preferred_element_type=jnp.float32)
            value = product.astype(jnp.bfloat16).astype(jnp.float32) + bias_ref[:, at]
            codes[me, here, at] = jnp.maximum(value, 0.0).astype(jnp.bfloat16)
            return carry

        lax.fori_loop(0, columns, column, 0)

    def home_features(kind):
        here = region(kind, chip, 0, sizes[kind])

        def column(n, carry):
            at = pl.ds(pl.multiple_of(n * column_tile, column_tile), column_tile)
            first = jnp.dot(
                codes[me, here], dec[me, :, at], preferred_element_type=jnp.float32
            )
            second = jnp.dot(
                codes[twin, here], dec[twin, :, at], preferred_element_type=jnp.float32
            )
            part[here, at] = first + second
            return carry

        lax.fori_loop(0, columns, column, 0)

    def finish(p):
        kind, start, count = pieces[p]
        here = region(kind, other, start, count)

        def add(owners, span):
            def column(n, carry):
                at = pl.ds(pl.multiple_of(n * span, span), span)
                total = part[here, at]
                for f in owners:
                    total += jnp.dot(
                        codes[f, here], dec[f, :, at], preferred_element_type=jnp.float32
                    )
                part[here, at] = total
                return carry

            lax.fori_loop(0, width // span, column, 0)

        t2(peer, p, other).wait_recv()
        t3(peer, p).start()
        if p == len(pieces) - 1:
            add([peer], width)
            t3(peer_twin, p).wait_recv()
            add([peer_twin], width)
        else:
            t3(peer_twin, p).wait_recv()
            add([peer, peer_twin], column_tile)
        whole = part[here].astype(jnp.bfloat16)
        summed[here] = whole
        error = (
            whole.astype(jnp.float32)
            + dec_bias_ref[...]
            - packed_targets[here].astype(jnp.float32)
        )
        live = jnp.concatenate([keep[here]] * (width // keep.shape[1]), axis=1)
        residual[here] = jnp.where(live > 0.0, error, 0.0).astype(jnp.bfloat16)

    load_live.wait()
    load_bias.wait()
    load_dec_bias.wait()
    load_act.wait()
    s1(1 - core).wait_recv()
    twin_tiles = live_ref[base + twin] + TILE - 1 >> 4
    for i in range(spare):
        own = core * block_tiles + sent - 1 - i
        theirs = (1 - core) * block_tiles + sent + i
        spill[spare - 1 - i] = acts_home[own + step(twin_tiles - sent - i) * (theirs - own)]
    for h in range(1, len(act_cuts)):
        s2(h).start()
    load_targets.wait()
    pack(acts_home, chip)
    load_enc.wait()
    encode(0)
    send(0)
    load_dec.wait()
    t1(twin, 0).wait_recv()
    home_features(0)

    for h in range(len(act_cuts)):
        s2(h).wait_recv()
    s3(core).start()
    s3(1 - core).wait_recv()
    pack(acts_away, other)
    encode(1)
    send(1)
    if rest:
        pack_rest()
        encode(2)
        send(2)
    for kind in kinds[1:]:
        t1(twin, kind).wait_recv()
        home_features(kind)
    for p in range(len(pieces)):
        finish(p)

    s1(core).wait_send()
    for h in range(len(act_cuts)):
        s2(h).wait_send()
    s3(core).wait_send()
    for kind in kinds:
        t1(me, kind).wait_send()
    for p in range(len(pieces)):
        t2(me, p, chip).wait_send()
        t3(peer, p).wait_send()


def choice_kernel(sizes, live_ref, choice_ref):
    choice = 0
    for group in range(0, live_ref.shape[0], 4):
        counts = [live_ref[group + b] + TILE - 1 >> 4 for b in range(4)]
        most = jnp.maximum(counts[0] + counts[1], counts[2] + counts[3])
        missed = sum(
            step(sum(counts) - tiles) | step(most - 2 * sent) for tiles, sent in sizes[:-1]
        )
        choice = jnp.maximum(choice, missed)
    choice_ref[0] = choice


def gradient_kernel(
    span,
    early,
    live_ref,
    codes_ref,
    residual_ref,
    summed_ref,
    bias_ref,
    rebuilt_hbm,
    grad_hbm,
    grad,
    rebuilt,
    sem,
):
    owners, width = codes_ref.shape[0], codes_ref.shape[2]
    block_tiles = rebuilt.shape[0] // TILE // 4
    base = lax.axis_index("blk") // 4 * 4
    per = width // span

    def out(f, i):
        at = pl.ds(pl.multiple_of(i * span, span), span)
        return pltpu.make_async_copy(grad.at[f, at], grad_hbm.at[f, at], sem.at[f * per + i])

    def block(f, i):
        at = pl.ds(i * span, span)
        grad[f, at] = lax.dot_general(
            codes_ref[f, :, at],
            residual_ref[...],
            (((0,), (0,)), ((), ())),
            preferred_element_type=jnp.float32,
        )
        out(f, i).start()

    counts = [live_ref[base + b] + TILE - 1 >> 4 for b in range(4)]
    first_extra = jnp.maximum(counts[0] + counts[1] - early // TILE, 0)

    def spread(b, s):
        live = live_ref[base + b]
        chip = b // 2
        k = b % 2 * (live_ref[base + b - b % 2] + TILE - 1 >> 4) + s
        place = jnp.where(
            k < early // TILE,
            chip * (early // TILE) + k,
            early // TILE + chip * first_extra + k,
        )
        place = jnp.where(TILE * s < live, place, 0)
        value = summed_ref[pl.ds(pl.multiple_of(place * TILE, TILE), TILE)].astype(jnp.float32)
        row = TILE * s + lax.broadcasted_iota(jnp.int32, value.shape, 0)
        at = pl.ds(pl.multiple_of((b * block_tiles + s) * TILE, TILE), TILE)
        rebuilt[at] = jnp.where(row < live, value, 0.0) + bias_ref[...]

    def give(b):
        at = pl.ds(pl.multiple_of(b * block_tiles * TILE, TILE), block_tiles * TILE)
        return pltpu.make_async_copy(rebuilt.at[at], rebuilt_hbm.at[at], sem.at[owners * per + b])

    def owner(f, carry):
        for i in range(per):
            block(f, i)
            for s in range(block_tiles * i // per, block_tiles * (i + 1) // per):
                spread(f, s)
        give(f).start()
        return carry

    lax.fori_loop(0, 4, owner, 0)

    def ended(i, carry):
        out(i // per, i % per).wait()
        return carry

    lax.fori_loop(0, owners * per, ended, 0)
    for b in range(4):
        give(b).wait()


def packed_tiles(
    order,
    tiles,
    sent,
    activations,
    live_rows,
    encoder_weight,
    encoder_bias,
    decoder_weight,
    decoder_bias,
    targets,
):
    rows, depth = activations.shape
    features = encoder_weight.shape[1]
    width = decoder_weight.shape[2]
    tokens = targets.shape[0]
    total = TILE * tiles
    early = total - 2 * rows
    block_tiles = rows // TILE
    spare = block_tiles - sent
    pieces = pieces_of(early, total - 2 * early)
    lanes = min(128, width)
    any_space = pl.BlockSpec(memory_space=pl.ANY)
    stay = functools.partial(pltpu.with_memory_space_constraint, memory_space=pltpu.HBM)
    in_vmem = pl.BlockSpec(memory_space=pltpu.VMEM)
    in_smem = pl.BlockSpec(memory_space=pltpu.SMEM)
    in_hbm = pl.BlockSpec(memory_space=pltpu.HBM)
    dma = pltpu.SemaphoreType.DMA
    bf16 = jnp.bfloat16
    f32 = jnp.float32
    codes, residual, summed = pl.pallas_call(
        functools.partial(gather_kernel, sent, early, pieces),
        out_shape=(
            pltpu.VMEM((4, total, features), bf16),
            pltpu.VMEM((total, width), bf16),
            pltpu.VMEM((total, width), bf16),
        ),
        in_specs=[in_hbm] * 7,
        out_specs=(in_vmem, in_vmem, in_vmem),
        scratch_shapes=[
            pltpu.VMEM((2 * block_tiles, TILE, depth), bf16),
            pltpu.VMEM((2 * sent, TILE, depth), bf16),
            pltpu.VMEM((max(spare, 1), TILE, depth), bf16),
            pltpu.VMEM((total, depth), bf16),
            pltpu.VMEM((depth, features), bf16),
            pltpu.VMEM((4, features, width), bf16),
            pltpu.VMEM((total, width), f32),
            pltpu.VMEM((4 * block_tiles, TILE, width), bf16),
            pltpu.VMEM((total, width), bf16),
            pltpu.VMEM((total, lanes), f32),
            pltpu.SMEM(live_rows.shape, jnp.int32),
            pltpu.VMEM((1, features), f32),
            pltpu.VMEM((1, width), f32),
            dma((7,)),
            dma((1,)),
            dma((1,)),
            dma((2,)),
            dma((2,)),
            dma((1,)),
            dma((1,)),
            dma((3,)),
            dma((3,)),
            dma((len(pieces),)),
            dma((len(pieces),)),
            dma((len(pieces),)),
            dma((len(pieces),)),
        ],
        compiler_params=pltpu.CompilerParams(
            collective_id=order, has_side_effects=True, vmem_limit_bytes=44 * 1024 * 1024
        ),
        name=f"gather_codes_{tiles}_{sent}",
    )(
        activations.reshape(block_tiles, TILE, depth),
        stay(live_rows),
        encoder_weight,
        stay(encoder_bias[None, :]),
        decoder_weight,
        stay(decoder_bias[None, :]),
        targets.reshape(4 * block_tiles, TILE, width),
    )

    span = min(256, features)
    rebuilt, grad = pl.pallas_call(
        functools.partial(gradient_kernel, span, early),
        out_shape=(
            jax.ShapeDtypeStruct((tokens, width), f32),
            jax.ShapeDtypeStruct((4, features, width), f32),
        ),
        in_specs=[in_smem, in_vmem, in_vmem, in_vmem, in_vmem],
        out_specs=(any_space, any_space),
        scratch_shapes=[
            pltpu.VMEM((4, features, width), f32),
            pltpu.VMEM((tokens, width), f32),
            dma((4 * (features // span) + 4,)),
        ],
        compiler_params=pltpu.CompilerParams(vmem_limit_bytes=44 * 1024 * 1024),
        name=f"gradient_{tiles}_{sent}",
    )(live_rows, codes, residual, summed, decoder_bias[None, :])
    return rebuilt, grad


def four_owners(activations, live_rows, *operands):
    rows = activations.shape[0]
    if rows % TILE:
        return general(activations, live_rows, *operands)
    block_tiles = rows // TILE
    fewer = max(block_tiles * 9 // 10, block_tiles // 2 + 1)
    shares = ((9, fewer), (12, fewer), (12, block_tiles), (15, block_tiles), (20, block_tiles))
    sizes = sorted({(2 * block_tiles + max(1, block_tiles * k // 10), sent) for k, sent in shares})
    in_smem = pl.BlockSpec(memory_space=pltpu.SMEM)
    choice = pl.pallas_call(
        functools.partial(choice_kernel, sizes),
        out_shape=jax.ShapeDtypeStruct((1,), jnp.int32),
        in_specs=[in_smem],
        out_specs=in_smem,
        name="choice",
    )(live_rows)
    return lax.switch(
        choice[0],
        [functools.partial(packed_tiles, order, *size) for order, size in enumerate(sizes)],
        activations,
        live_rows,
        *operands,
    )


def from_partner(shard, axis, distance):
    return lax.ppermute(shard, axis, [(i, i ^ 1 << distance) for i in range(lax.axis_size(axis))])


def group_rows(block, levels, position):
    for bit in range(levels):
        other = from_partner(block, "blk", bit)
        upper = position >> bit & 1 == 1
        block = jnp.where(
            upper, jnp.concatenate([other, block], 0), jnp.concatenate([block, other], 0)
        )
    return block


def general(
    activations, live_rows, encoder_weight, encoder_bias, decoder_weight, decoder_bias, targets
):
    owners = lax.axis_size("blk") // G
    levels = owners.bit_length() - 1
    shares = lax.axis_size("feat")
    position = lax.axis_index("blk")
    share_index = lax.axis_index("feat")
    group_index = position // owners
    tok_rows = activations.shape[0]
    counts = lax.dynamic_slice_in_dim(live_rows, group_index * owners, owners)
    positions = jnp.arange(tok_rows, dtype=jnp.int32)
    live_mask = (positions[None, :] < counts[:, None]).astype(jnp.float32).reshape(-1)
    gathered = group_rows(activations, levels, position)
    per_share = encoder_weight.shape[1] // shares
    bias_share = lax.dynamic_slice_in_dim(encoder_bias, share_index * per_share, per_share)
    columns = encoder_weight
    whole = lax.psum(
        lax.dot_general(
            columns, gathered, (((0,), (1,)), ((), ())), preferred_element_type=jnp.float32
        ).astype(jnp.bfloat16),
        "feat",
    ).astype(jnp.float32)
    preact = lax.dynamic_slice_in_dim(whole, share_index * per_share, per_share, 0)
    codes_by_feature = (jax.nn.relu(preact + bias_share[:, None]) * live_mask[None, :]).astype(
        jnp.bfloat16
    )
    codes_all = group_rows(codes_by_feature, levels, position)
    decoder_rows = decoder_weight.reshape(-1, decoder_weight.shape[2])
    block_rows = gathered.shape[0] // shares
    columns = codes_all
    summed = lax.psum_scatter(
        lax.dot_general(
            columns, decoder_rows, (((0,), (0,)), ((), ())), preferred_element_type=jnp.float32
        ).astype(jnp.bfloat16),
        "feat",
        scatter_dimension=0,
        tiled=True,
    ).astype(jnp.float32)
    rebuilt = summed + decoder_bias[None, :]
    mask_block = lax.dynamic_slice_in_dim(live_mask, share_index * block_rows, block_rows)
    residual = ((rebuilt - targets.astype(jnp.float32)) * mask_block[:, None]).astype(jnp.bfloat16)
    columns = codes_all
    gradient = jnp.dot(
        columns,
        lax.all_gather(residual, "feat", axis=0, tiled=True),
        preferred_element_type=jnp.float32,
    )
    return (rebuilt, gradient.reshape(decoder_weight.shape))


def solution(mesh):
    in_specs = (
        P("blk", "feat"),
        P(),
        P("feat", "blk"),
        P("blk"),
        P(None, "feat", "blk"),
        P("blk"),
        P("feat", "blk"),
    )
    out_specs = (P("feat", "blk"), P(None, "feat", "blk"))
    fused = mesh.shape["blk"] // G == 4 and mesh.shape["feat"] == 1
    return jax.shard_map(
        four_owners if fused else general,
        mesh=mesh,
        in_specs=in_specs,
        out_specs=out_specs,
        check_vma=False,
    )
```

```python
import functools

import jax
import jax.numpy as jnp
from jax import lax
from jax.experimental import pallas as pl
from jax.experimental.pallas import tpu as pltpu
from jax.sharding import PartitionSpec as P

G = 8
TILE = 16
MESH = pl.DeviceIdType.MESH


def cuts(rows, parts):
    if rows % 16 or rows // 16 < len(parts):
        return [(0, rows)]
    tiles, total, edges = rows // 16, sum(parts), [0]
    for k in range(1, len(parts)):
        edges.append(max(edges[-1] + 1, tiles * sum(parts[:k]) // total))
    edges.append(tiles)
    return [(16 * a, 16 * (b - a)) for a, b in zip(edges[:-1], edges[1:])]


def pieces_of(early, rest):
    first = [(0, *cut) for cut in cuts(early, (1,))]
    if rest:
        late = [(1, *cut) for cut in cuts(early, (1,))]
        return first + late + [(2, *cut) for cut in cuts(rest, (1,))]
    return first + [(1, *cut) for cut in cuts(early, (1, 1))]


def step(count):
    return jnp.clip(count, 0, 1)


def tile_of(first_live, second_live, tiles, k):
    first = first_live + TILE - 1 >> 4
    second = second_live + TILE - 1 >> 4
    late = 1 - step(first - k)
    inside = jnp.minimum(k - late * first, tiles - 1)
    live = first_live + late * (second_live - first_live) - TILE * inside
    return late, inside, step(first + second - k) * live


def slot_of(late, inside, sent):
    over = step(inside - sent + 1)
    return (late + over - 2 * late * over) * sent + inside + over * (2 * sent - 1 - 2 * inside)


def gather_kernel(
    sent,
    early,
    pieces,
    act_hbm,
    live_hbm,
    enc_hbm,
    bias_hbm,
    dec_hbm,
    dec_bias_hbm,
    targets_hbm,
    codes,
    residual,
    summed,
    acts_home,
    acts_away,
    spill,
    packed,
    enc,
    dec,
    part,
    targets,
    packed_targets,
    keep,
    live_ref,
    bias_ref,
    dec_bias_ref,
    load_sem,
    s1_send,
    s1_recv,
    s2_send,
    s2_recv,
    s3_send,
    s3_recv,
    t1_send,
    t1_recv,
    t2_send,
    t2_recv,
    t3_send,
    t3_recv,
):
    position = lax.axis_index("blk")
    share = lax.axis_index("feat")
    base = position // 4 * 4
    me = position % 4
    core = me % 2
    home = me - core
    away = 2 - home
    chip = home // 2
    other = 1 - chip
    twin = home + 1 - core
    peer = away + core
    peer_twin = away + 1 - core
    on_chip = (base + twin, share)
    across = (base + peer, share)

    block_tiles = act_hbm.shape[0]
    spare = block_tiles - sent
    act_cuts = [(0, sent - spare)] + [(sent - spare, spare)] * (spare > 0)
    total = codes.shape[1]
    rest = total - 2 * early
    width = enc.shape[1]
    column_tile = min(256, width)
    columns = width // column_tile

    def own_tiles(at_core, start, count):
        return pl.ds(at_core * block_tiles + start, count)

    load_act = pltpu.make_async_copy(
        act_hbm, acts_home.at[own_tiles(core, 0, block_tiles)], load_sem.at[0]
    )
    load_enc = pltpu.make_async_copy(enc_hbm, enc, load_sem.at[1])
    load_dec = pltpu.make_async_copy(dec_hbm, dec, load_sem.at[2])
    load_targets = pltpu.make_async_copy(targets_hbm, targets, load_sem.at[3])
    load_live = pltpu.make_async_copy(live_hbm, live_ref, load_sem.at[4])
    load_bias = pltpu.make_async_copy(bias_hbm, bias_ref, load_sem.at[5])
    load_dec_bias = pltpu.make_async_copy(dec_bias_hbm, dec_bias_ref, load_sem.at[6])
    load_live.start()
    load_bias.start()
    load_act.start()
    load_enc.start()
    load_dec_bias.start()

    barrier = pltpu.get_barrier_semaphore()
    for neighbour in (on_chip, across):
        pl.semaphore_signal(barrier, inc=1, device_id=neighbour, device_id_type=MESH)
    pl.semaphore_wait(barrier, 2)

    def remote(src, dst, send, recv, to):
        return pltpu.make_async_remote_copy(
            src_ref=src,
            dst_ref=dst,
            send_sem=send,
            recv_sem=recv,
            device_id=to,
            device_id_type=MESH,
        )

    def s1(at_core):
        ref = acts_home.at[own_tiles(at_core, 0, block_tiles)]
        return remote(act_hbm, ref, s1_send.at[0], s1_recv.at[0], on_chip)

    def s2(h):
        at, count = act_cuts[h]
        src = spill if h else act_hbm.at[pl.ds(at, count)]
        ref = acts_away.at[pl.ds(core * sent + at, count)]
        return remote(src, ref, s2_send.at[h], s2_recv.at[h], across)

    def s3(at_core):
        ref = acts_away.at[pl.ds(at_core * sent, sent)]
        return remote(ref, ref, s3_send.at[0], s3_recv.at[0], on_chip)

    def region(kind, of_chip, start, count):
        first = (of_chip * early, (1 - of_chip) * early, 2 * early)[kind]
        return pl.ds(pl.multiple_of(first + start, TILE), count)

    sizes = (early, early, rest)
    kinds = (0, 1, 2) if rest else (0, 1)

    def t1(f, kind):
        ref = codes.at[f, region(kind, chip, 0, sizes[kind])]
        return remote(ref, ref, t1_send.at[kind], t1_recv.at[kind], on_chip)

    def t2(f, p, of_chip):
        kind, start, count = pieces[p]
        ref = codes.at[f, region(kind, of_chip, start, count)]
        return remote(ref, ref, t2_send.at[p], t2_recv.at[p], across)

    def t3(f, p):
        kind, start, count = pieces[p]
        ref = codes.at[f, region(kind, other, start, count)]
        return remote(ref, ref, t3_send.at[p], t3_recv.at[p], on_chip)

    def send(kind):
        t1(me, kind).start()
        for p, piece in enumerate(pieces):
            if piece[0] == kind:
                t2(me, p, chip).start()

    s2(0).start()
    s1(core).start()
    load_dec.start()
    load_targets.start()

    def mark(at, live, where):
        keep[at] = (lax.broadcasted_iota(jnp.int32, (TILE, keep.shape[1]), 0) < live).astype(
            jnp.float32
        )
        packed_targets[at] = targets[where]

    def pack(acts, of_chip):
        first_live = live_ref[base + 2 * of_chip]
        second_live = live_ref[base + 2 * of_chip + 1]

        def one(k, carry):
            late, inside, live = tile_of(first_live, second_live, block_tiles, k)
            where = late * block_tiles + inside
            at = pl.ds(pl.multiple_of(of_chip * early + k * TILE, TILE), TILE)
            packed[at] = acts[slot_of(late, inside, sent) if acts is acts_away else where]
            mark(at, live, of_chip * 2 * block_tiles + where)
            return carry

        lax.fori_loop(0, early // TILE, one, 0)

    def pack_rest():
        lives = [live_ref[base + b] for b in range(4)]
        first_extra = jnp.maximum(
            (lives[0] + TILE - 1 >> 4) + (lives[1] + TILE - 1 >> 4) - early // TILE, 0
        )

        def one(k, carry):
            from_first = step(first_extra - k)
            index = early // TILE + k - (1 - from_first) * first_extra
            late0, inside0, live0 = tile_of(lives[0], lives[1], block_tiles, index)
            late1, inside1, live1 = tile_of(lives[2], lives[3], block_tiles, index)
            where0 = late0 * block_tiles + inside0
            where1 = late1 * block_tiles + inside1
            slot0 = slot_of(late0, inside0, sent)
            slot1 = slot_of(late1, inside1, sent)
            where_home = where0 + chip * (where1 - where0)
            where_away = slot1 + chip * (slot0 - slot1)
            at = pl.ds(pl.multiple_of(2 * early + k * TILE, TILE), TILE)
            mine = jnp.full((TILE, acts_home.shape[2]), from_first + chip, jnp.int32) == 1
            packed[at] = jnp.where(mine, acts_home[where_home], acts_away[where_away])
            mark(
                at,
                live1 + from_first * (live0 - live1),
                where1 + 2 * block_tiles + from_first * (where0 - where1 - 2 * block_tiles),
            )
            return carry

        lax.fori_loop(0, rest // TILE, one, 0)

    def encode(kind):
        here = region(kind, chip, 0, sizes[kind])

        def column(n, carry):
            at = pl.ds(pl.multiple_of(n * column_tile, column_tile), column_tile)
            product = jnp.dot(packed[here], enc[:, at], preferred_element_type=jnp.float32)
            value = product.astype(jnp.bfloat16).astype(jnp.float32) + bias_ref[:, at]
            codes[me, here, at] = jnp.maximum(value, 0.0).astype(jnp.bfloat16)
            return carry

        lax.fori_loop(0, columns, column, 0)

    def home_features(kind):
        here = region(kind, chip, 0, sizes[kind])

        def column(n, carry):
            at = pl.ds(pl.multiple_of(n * column_tile, column_tile), column_tile)
            first = jnp.dot(
                codes[me, here], dec[me, :, at], preferred_element_type=jnp.float32
            )
            second = jnp.dot(
                codes[twin, here], dec[twin, :, at], preferred_element_type=jnp.float32
            )
            part[here, at] = first + second
            return carry

        lax.fori_loop(0, columns, column, 0)

    def finish(p):
        kind, start, count = pieces[p]
        here = region(kind, other, start, count)

        def add(owners, span):
            def column(n, carry):
                at = pl.ds(pl.multiple_of(n * span, span), span)
                total = part[here, at]
                for f in owners:
                    total += jnp.dot(
                        codes[f, here], dec[f, :, at], preferred_element_type=jnp.float32
                    )
                part[here, at] = total
                return carry

            lax.fori_loop(0, width // span, column, 0)

        t2(peer, p, other).wait_recv()
        t3(peer, p).start()
        if p == len(pieces) - 1:
            add([peer], width)
            t3(peer_twin, p).wait_recv()
            add([peer_twin], width)
        else:
            t3(peer_twin, p).wait_recv()
            add([peer, peer_twin], min(512, width) if p else column_tile)
        whole = part[here].astype(jnp.bfloat16)
        summed[here] = whole
        error = (
            whole.astype(jnp.float32)
            + dec_bias_ref[...]
            - packed_targets[here].astype(jnp.float32)
        )
        live = jnp.concatenate([keep[here]] * (width // keep.shape[1]), axis=1)
        residual[here] = jnp.where(live > 0.0, error, 0.0).astype(jnp.bfloat16)

    load_live.wait()
    load_bias.wait()
    load_dec_bias.wait()
    load_act.wait()
    s1(1 - core).wait_recv()
    twin_tiles = live_ref[base + twin] + TILE - 1 >> 4
    for i in range(spare):
        own = core * block_tiles + sent - 1 - i
        theirs = (1 - core) * block_tiles + sent + i
        spill[spare - 1 - i] = acts_home[own + step(twin_tiles - sent - i) * (theirs - own)]
    for h in range(1, len(act_cuts)):
        s2(h).start()
    load_targets.wait()
    pack(acts_home, chip)
    load_enc.wait()
    encode(0)
    send(0)
    load_dec.wait()
    t1(twin, 0).wait_recv()
    home_features(0)

    for h in range(len(act_cuts)):
        s2(h).wait_recv()
    s3(core).start()
    s3(1 - core).wait_recv()
    pack(acts_away, other)
    encode(1)
    send(1)
    if rest:
        pack_rest()
        encode(2)
        send(2)
    for kind in kinds[1:]:
        t1(twin, kind).wait_recv()
        home_features(kind)
    for p in range(len(pieces)):
        finish(p)

    s1(core).wait_send()
    for h in range(len(act_cuts)):
        s2(h).wait_send()
    s3(core).wait_send()
    for kind in kinds:
        t1(me, kind).wait_send()
    for p in range(len(pieces)):
        t2(me, p, chip).wait_send()
        t3(peer, p).wait_send()


def choice_kernel(sizes, live_ref, choice_ref):
    choice = 0
    for group in range(0, live_ref.shape[0], 4):
        counts = [live_ref[group + b] + TILE - 1 >> 4 for b in range(4)]
        most = jnp.maximum(counts[0] + counts[1], counts[2] + counts[3])
        missed = sum(
            step(sum(counts) - tiles) | step(most - 2 * sent) for tiles, sent in sizes[:-1]
        )
        choice = jnp.maximum(choice, missed)
    choice_ref[0] = choice


def gradient_kernel(
    span,
    early,
    live_ref,
    codes_ref,
    residual_ref,
    summed_ref,
    bias_ref,
    rebuilt_hbm,
    grad_hbm,
    grad,
    rebuilt,
    sem,
):
    owners, width = codes_ref.shape[0], codes_ref.shape[2]
    block_tiles = rebuilt.shape[0] // TILE // 4
    base = lax.axis_index("blk") // 4 * 4
    per = width // span

    def out(f, i):
        at = pl.ds(pl.multiple_of(i * span, span), span)
        return pltpu.make_async_copy(grad.at[f, at], grad_hbm.at[f, at], sem.at[f * per + i])

    def block(f, i):
        at = pl.ds(i * span, span)
        grad[f, at] = lax.dot_general(
            codes_ref[f, :, at],
            residual_ref[...],
            (((0,), (0,)), ((), ())),
            preferred_element_type=jnp.float32,
        )
        out(f, i).start()

    counts = [live_ref[base + b] + TILE - 1 >> 4 for b in range(4)]
    first_extra = jnp.maximum(counts[0] + counts[1] - early // TILE, 0)

    def spread(b, s):
        live = live_ref[base + b]
        chip = b // 2
        k = b % 2 * (live_ref[base + b - b % 2] + TILE - 1 >> 4) + s
        place = jnp.where(
            k < early // TILE,
            chip * (early // TILE) + k,
            early // TILE + chip * first_extra + k,
        )
        place = jnp.where(TILE * s < live, place, 0)
        value = summed_ref[pl.ds(pl.multiple_of(place * TILE, TILE), TILE)].astype(jnp.float32)
        row = TILE * s + lax.broadcasted_iota(jnp.int32, value.shape, 0)
        at = pl.ds(pl.multiple_of((b * block_tiles + s) * TILE, TILE), TILE)
        rebuilt[at] = jnp.where(row < live, value, 0.0) + bias_ref[...]

    def give(b):
        at = pl.ds(pl.multiple_of(b * block_tiles * TILE, TILE), block_tiles * TILE)
        return pltpu.make_async_copy(rebuilt.at[at], rebuilt_hbm.at[at], sem.at[owners * per + b])

    def owner(f, carry):
        for i in range(per):
            block(f, i)
            for s in range(block_tiles * i // per, block_tiles * (i + 1) // per):
                spread(f, s)
        give(f).start()
        return carry

    lax.fori_loop(0, 4, owner, 0)

    def ended(i, carry):
        out(i // per, i % per).wait()
        return carry

    lax.fori_loop(0, owners * per, ended, 0)
    for b in range(4):
        give(b).wait()


def packed_tiles(
    order,
    tiles,
    sent,
    activations,
    live_rows,
    encoder_weight,
    encoder_bias,
    decoder_weight,
    decoder_bias,
    targets,
):
    rows, depth = activations.shape
    features = encoder_weight.shape[1]
    width = decoder_weight.shape[2]
    tokens = targets.shape[0]
    total = TILE * tiles
    early = total - 2 * rows
    block_tiles = rows // TILE
    spare = block_tiles - sent
    pieces = pieces_of(early, total - 2 * early)
    lanes = min(128, width)
    any_space = pl.BlockSpec(memory_space=pl.ANY)
    stay = functools.partial(pltpu.with_memory_space_constraint, memory_space=pltpu.HBM)
    in_vmem = pl.BlockSpec(memory_space=pltpu.VMEM)
    in_smem = pl.BlockSpec(memory_space=pltpu.SMEM)
    in_hbm = pl.BlockSpec(memory_space=pltpu.HBM)
    dma = pltpu.SemaphoreType.DMA
    bf16 = jnp.bfloat16
    f32 = jnp.float32
    codes, residual, summed = pl.pallas_call(
        functools.partial(gather_kernel, sent, early, pieces),
        out_shape=(
            pltpu.VMEM((4, total, features), bf16),
            pltpu.VMEM((total, width), bf16),
            pltpu.VMEM((total, width), bf16),
        ),
        in_specs=[in_hbm] * 7,
        out_specs=(in_vmem, in_vmem, in_vmem),
        scratch_shapes=[
            pltpu.VMEM((2 * block_tiles, TILE, depth), bf16),
            pltpu.VMEM((2 * sent, TILE, depth), bf16),
            pltpu.VMEM((max(spare, 1), TILE, depth), bf16),
            pltpu.VMEM((total, depth), bf16),
            pltpu.VMEM((depth, features), bf16),
            pltpu.VMEM((4, features, width), bf16),
            pltpu.VMEM((total, width), f32),
            pltpu.VMEM((4 * block_tiles, TILE, width), bf16),
            pltpu.VMEM((total, width), bf16),
            pltpu.VMEM((total, lanes), f32),
            pltpu.SMEM(live_rows.shape, jnp.int32),
            pltpu.VMEM((1, features), f32),
            pltpu.VMEM((1, width), f32),
            dma((7,)),
            dma((1,)),
            dma((1,)),
            dma((2,)),
            dma((2,)),
            dma((1,)),
            dma((1,)),
            dma((3,)),
            dma((3,)),
            dma((len(pieces),)),
            dma((len(pieces),)),
            dma((len(pieces),)),
            dma((len(pieces),)),
        ],
        compiler_params=pltpu.CompilerParams(
            collective_id=order, has_side_effects=True, vmem_limit_bytes=44 * 1024 * 1024
        ),
        name=f"gather_codes_{tiles}_{sent}",
    )(
        activations.reshape(block_tiles, TILE, depth),
        stay(live_rows),
        encoder_weight,
        stay(encoder_bias[None, :]),
        decoder_weight,
        stay(decoder_bias[None, :]),
        targets.reshape(4 * block_tiles, TILE, width),
    )

    span = min(256, features)
    rebuilt, grad = pl.pallas_call(
        functools.partial(gradient_kernel, span, early),
        out_shape=(
            jax.ShapeDtypeStruct((tokens, width), f32),
            jax.ShapeDtypeStruct((4, features, width), f32),
        ),
        in_specs=[in_smem, in_vmem, in_vmem, in_vmem, in_vmem],
        out_specs=(any_space, any_space),
        scratch_shapes=[
            pltpu.VMEM((4, features, width), f32),
            pltpu.VMEM((tokens, width), f32),
            dma((4 * (features // span) + 4,)),
        ],
        compiler_params=pltpu.CompilerParams(vmem_limit_bytes=44 * 1024 * 1024),
        name=f"gradient_{tiles}_{sent}",
    )(live_rows, codes, residual, summed, decoder_bias[None, :])
    return rebuilt, grad


def four_owners(activations, live_rows, *operands):
    rows = activations.shape[0]
    if rows % TILE:
        return general(activations, live_rows, *operands)
    block_tiles = rows // TILE
    fewer = max(block_tiles * 9 // 10, block_tiles // 2 + 1)
    shares = ((9, fewer), (12, fewer), (12, block_tiles), (15, block_tiles), (20, block_tiles))
    sizes = sorted({(2 * block_tiles + max(1, block_tiles * k // 10), sent) for k, sent in shares})
    in_smem = pl.BlockSpec(memory_space=pltpu.SMEM)
    choice = pl.pallas_call(
        functools.partial(choice_kernel, sizes),
        out_shape=pltpu.SMEM((1,), jnp.int32),
        in_specs=[in_smem],
        out_specs=in_smem,
        name="choice",
    )(live_rows)
    return lax.switch(
        choice[0],
        [functools.partial(packed_tiles, order, *size) for order, size in enumerate(sizes)],
        activations,
        live_rows,
        *operands,
    )


def from_partner(shard, axis, distance):
    return lax.ppermute(shard, axis, [(i, i ^ 1 << distance) for i in range(lax.axis_size(axis))])


def group_rows(block, levels, position):
    for bit in range(levels):
        other = from_partner(block, "blk", bit)
        upper = position >> bit & 1 == 1
        block = jnp.where(
            upper, jnp.concatenate([other, block], 0), jnp.concatenate([block, other], 0)
        )
    return block


def general(
    activations, live_rows, encoder_weight, encoder_bias, decoder_weight, decoder_bias, targets
):
    owners = lax.axis_size("blk") // G
    levels = owners.bit_length() - 1
    shares = lax.axis_size("feat")
    position = lax.axis_index("blk")
    share_index = lax.axis_index("feat")
    group_index = position // owners
    tok_rows = activations.shape[0]
    counts = lax.dynamic_slice_in_dim(live_rows, group_index * owners, owners)
    positions = jnp.arange(tok_rows, dtype=jnp.int32)
    live_mask = (positions[None, :] < counts[:, None]).astype(jnp.float32).reshape(-1)
    gathered = group_rows(activations, levels, position)
    per_share = encoder_weight.shape[1] // shares
    bias_share = lax.dynamic_slice_in_dim(encoder_bias, share_index * per_share, per_share)
    columns = encoder_weight
    whole = lax.psum(
        lax.dot_general(
            columns, gathered, (((0,), (1,)), ((), ())), preferred_element_type=jnp.float32
        ).astype(jnp.bfloat16),
        "feat",
    ).astype(jnp.float32)
    preact = lax.dynamic_slice_in_dim(whole, share_index * per_share, per_share, 0)
    codes_by_feature = (jax.nn.relu(preact + bias_share[:, None]) * live_mask[None, :]).astype(
        jnp.bfloat16
    )
    codes_all = group_rows(codes_by_feature, levels, position)
    decoder_rows = decoder_weight.reshape(-1, decoder_weight.shape[2])
    block_rows = gathered.shape[0] // shares
    columns = codes_all
    summed = lax.psum_scatter(
        lax.dot_general(
            columns, decoder_rows, (((0,), (0,)), ((), ())), preferred_element_type=jnp.float32
        ).astype(jnp.bfloat16),
        "feat",
        scatter_dimension=0,
        tiled=True,
    ).astype(jnp.float32)
    rebuilt = summed + decoder_bias[None, :]
    mask_block = lax.dynamic_slice_in_dim(live_mask, share_index * block_rows, block_rows)
    residual = ((rebuilt - targets.astype(jnp.float32)) * mask_block[:, None]).astype(jnp.bfloat16)
    columns = codes_all
    gradient = jnp.dot(
        columns,
        lax.all_gather(residual, "feat", axis=0, tiled=True),
        preferred_element_type=jnp.float32,
    )
    return (rebuilt, gradient.reshape(decoder_weight.shape))


def solution(mesh):
    in_specs = (
        P("blk", "feat"),
        P(),
        P("feat", "blk"),
        P("blk"),
        P(None, "feat", "blk"),
        P("blk"),
        P("feat", "blk"),
    )
    out_specs = (P("feat", "blk"), P(None, "feat", "blk"))
    fused = mesh.shape["blk"] // G == 4 and mesh.shape["feat"] == 1
    return jax.shard_map(
        four_owners if fused else general,
        mesh=mesh,
        in_specs=in_specs,
        out_specs=out_specs,
        check_vma=False,
    )
```

```python
import functools

import jax
import jax.numpy as jnp
from jax import lax
from jax.experimental import pallas as pl
from jax.experimental.pallas import tpu as pltpu
from jax.sharding import PartitionSpec as P

G = 8
TILE = 16
MESH = pl.DeviceIdType.MESH


def cuts(rows, parts):
    if rows % 16 or rows // 16 < len(parts):
        return [(0, rows)]
    tiles, total, edges = rows // 16, sum(parts), [0]
    for k in range(1, len(parts)):
        edges.append(max(edges[-1] + 1, tiles * sum(parts[:k]) // total))
    edges.append(tiles)
    return [(16 * a, 16 * (b - a)) for a, b in zip(edges[:-1], edges[1:])]


def pieces_of(early, rest):
    first = [(0, *cut) for cut in cuts(early, (1,))]
    if rest:
        late = [(1, *cut) for cut in cuts(early, (1,))]
        return first + late + [(2, *cut) for cut in cuts(rest, (1,))]
    return first + [(1, *cut) for cut in cuts(early, (1, 1))]


def step(count):
    return jnp.clip(count, 0, 1)


def tile_of(first_live, second_live, tiles, k):
    first = first_live + TILE - 1 >> 4
    second = second_live + TILE - 1 >> 4
    late = 1 - step(first - k)
    inside = jnp.minimum(k - late * first, tiles - 1)
    live = first_live + late * (second_live - first_live) - TILE * inside
    return late, inside, step(first + second - k) * live


def slot_of(late, inside, sent):
    over = step(inside - sent + 1)
    return (late + over - 2 * late * over) * sent + inside + over * (2 * sent - 1 - 2 * inside)


def gather_kernel(
    sent,
    early,
    pieces,
    act_hbm,
    live_hbm,
    enc_hbm,
    bias_hbm,
    dec_hbm,
    dec_bias_hbm,
    targets_hbm,
    codes,
    residual,
    summed,
    acts_home,
    acts_away,
    spill,
    packed,
    enc,
    dec,
    part,
    targets,
    packed_targets,
    keep,
    live_ref,
    bias_ref,
    dec_bias_ref,
    load_sem,
    s1_send,
    s1_recv,
    s2_send,
    s2_recv,
    s3_send,
    s3_recv,
    t1_send,
    t1_recv,
    t2_send,
    t2_recv,
    t3_send,
    t3_recv,
):
    position = lax.axis_index("blk")
    share = lax.axis_index("feat")
    base = position // 4 * 4
    me = position % 4
    core = me % 2
    home = me - core
    away = 2 - home
    chip = home // 2
    other = 1 - chip
    twin = home + 1 - core
    peer = away + core
    peer_twin = away + 1 - core
    on_chip = (base + twin, share)
    across = (base + peer, share)

    block_tiles = act_hbm.shape[0]
    spare = block_tiles - sent
    act_cuts = [(0, sent - spare)] + [(sent - spare, spare)] * (spare > 0)
    total = codes.shape[1]
    rest = total - 2 * early
    width = enc.shape[1]
    column_tile = min(256, width)
    columns = width // column_tile

    def own_tiles(at_core, start, count):
        return pl.ds(at_core * block_tiles + start, count)

    load_act = pltpu.make_async_copy(
        act_hbm, acts_home.at[own_tiles(core, 0, block_tiles)], load_sem.at[0]
    )
    load_enc = pltpu.make_async_copy(enc_hbm, enc, load_sem.at[1])
    load_dec = pltpu.make_async_copy(dec_hbm, dec, load_sem.at[2])
    load_targets = pltpu.make_async_copy(targets_hbm, targets, load_sem.at[3])
    load_live = pltpu.make_async_copy(live_hbm, live_ref, load_sem.at[4])
    load_bias = pltpu.make_async_copy(bias_hbm, bias_ref, load_sem.at[5])
    load_dec_bias = pltpu.make_async_copy(dec_bias_hbm, dec_bias_ref, load_sem.at[6])
    load_live.start()
    load_bias.start()
    load_act.start()
    load_enc.start()
    load_dec_bias.start()

    barrier = pltpu.get_barrier_semaphore()
    for neighbour in (on_chip, across):
        pl.semaphore_signal(barrier, inc=1, device_id=neighbour, device_id_type=MESH)
    pl.semaphore_wait(barrier, 2)

    def remote(src, dst, send, recv, to):
        return pltpu.make_async_remote_copy(
            src_ref=src,
            dst_ref=dst,
            send_sem=send,
            recv_sem=recv,
            device_id=to,
            device_id_type=MESH,
        )

    def s1(at_core):
        ref = acts_home.at[own_tiles(at_core, 0, block_tiles)]
        return remote(act_hbm, ref, s1_send.at[0], s1_recv.at[0], on_chip)

    def s2(h):
        at, count = act_cuts[h]
        src = spill if h else act_hbm.at[pl.ds(at, count)]
        ref = acts_away.at[pl.ds(core * sent + at, count)]
        return remote(src, ref, s2_send.at[h], s2_recv.at[h], across)

    def s3(at_core):
        ref = acts_away.at[pl.ds(at_core * sent, sent)]
        return remote(ref, ref, s3_send.at[0], s3_recv.at[0], on_chip)

    def region(kind, of_chip, start, count):
        first = (of_chip * early, (1 - of_chip) * early, 2 * early)[kind]
        return pl.ds(pl.multiple_of(first + start, TILE), count)

    sizes = (early, early, rest)
    kinds = (0, 1, 2) if rest else (0, 1)

    def t1(f, kind):
        ref = codes.at[f, region(kind, chip, 0, sizes[kind])]
        return remote(ref, ref, t1_send.at[kind], t1_recv.at[kind], on_chip)

    def t2(f, p, of_chip):
        kind, start, count = pieces[p]
        ref = codes.at[f, region(kind, of_chip, start, count)]
        return remote(ref, ref, t2_send.at[p], t2_recv.at[p], across)

    def t3(f, p):
        kind, start, count = pieces[p]
        ref = codes.at[f, region(kind, other, start, count)]
        return remote(ref, ref, t3_send.at[p], t3_recv.at[p], on_chip)

    def send(kind):
        t1(me, kind).start()
        for p, piece in enumerate(pieces):
            if piece[0] == kind:
                t2(me, p, chip).start()

    s2(0).start()
    s1(core).start()
    load_dec.start()
    load_targets.start()

    def mark(at, live, where):
        keep[at] = (lax.broadcasted_iota(jnp.int32, (TILE, keep.shape[1]), 0) < live).astype(
            jnp.float32
        )
        packed_targets[at] = targets[where]

    def pack(acts, of_chip):
        first_live = live_ref[base + 2 * of_chip]
        second_live = live_ref[base + 2 * of_chip + 1]

        def one(k, carry):
            late, inside, live = tile_of(first_live, second_live, block_tiles, k)
            where = late * block_tiles + inside
            at = pl.ds(pl.multiple_of(of_chip * early + k * TILE, TILE), TILE)
            packed[at] = acts[slot_of(late, inside, sent) if acts is acts_away else where]
            mark(at, live, of_chip * 2 * block_tiles + where)
            return carry

        lax.fori_loop(0, early // TILE, one, 0)

    def pack_rest():
        lives = [live_ref[base + b] for b in range(4)]
        first_extra = jnp.maximum(
            (lives[0] + TILE - 1 >> 4) + (lives[1] + TILE - 1 >> 4) - early // TILE, 0
        )

        def one(k, carry):
            from_first = step(first_extra - k)
            index = early // TILE + k - (1 - from_first) * first_extra
            late0, inside0, live0 = tile_of(lives[0], lives[1], block_tiles, index)
            late1, inside1, live1 = tile_of(lives[2], lives[3], block_tiles, index)
            where0 = late0 * block_tiles + inside0
            where1 = late1 * block_tiles + inside1
            slot0 = slot_of(late0, inside0, sent)
            slot1 = slot_of(late1, inside1, sent)
            where_home = where0 + chip * (where1 - where0)
            where_away = slot1 + chip * (slot0 - slot1)
            at = pl.ds(pl.multiple_of(2 * early + k * TILE, TILE), TILE)
            mine = jnp.full((TILE, acts_home.shape[2]), from_first + chip, jnp.int32) == 1
            packed[at] = jnp.where(mine, acts_home[where_home], acts_away[where_away])
            mark(
                at,
                live1 + from_first * (live0 - live1),
                where1 + 2 * block_tiles + from_first * (where0 - where1 - 2 * block_tiles),
            )
            return carry

        lax.fori_loop(0, rest // TILE, one, 0)

    def encode(kind):
        here = region(kind, chip, 0, sizes[kind])

        def column(n, carry):
            at = pl.ds(pl.multiple_of(n * column_tile, column_tile), column_tile)
            product = jnp.dot(packed[here], enc[:, at], preferred_element_type=jnp.float32)
            value = product.astype(jnp.bfloat16).astype(jnp.float32) + bias_ref[:, at]
            codes[me, here, at] = jnp.maximum(value, 0.0).astype(jnp.bfloat16)
            return carry

        lax.fori_loop(0, columns, column, 0)

    def home_features(kind):
        here = region(kind, chip, 0, sizes[kind])

        def column(n, carry):
            at = pl.ds(pl.multiple_of(n * column_tile, column_tile), column_tile)
            first = jnp.dot(
                codes[me, here], dec[me, :, at], preferred_element_type=jnp.float32
            )
            second = jnp.dot(
                codes[twin, here], dec[twin, :, at], preferred_element_type=jnp.float32
            )
            part[here, at] = first + second
            return carry

        lax.fori_loop(0, columns, column, 0)

    def finish(p):
        kind, start, count = pieces[p]
        here = region(kind, other, start, count)

        def add(owners, span):
            def column(n, carry):
                at = pl.ds(pl.multiple_of(n * span, span), span)
                total = part[here, at]
                for f in owners:
                    total += jnp.dot(
                        codes[f, here], dec[f, :, at], preferred_element_type=jnp.float32
                    )
                part[here, at] = total
                return carry

            lax.fori_loop(0, width // span, column, 0)

        t2(peer, p, other).wait_recv()
        t3(peer, p).start()
        if p == len(pieces) - 1:
            add([peer], width)
            t3(peer_twin, p).wait_recv()
            add([peer_twin], width)
        else:
            t3(peer_twin, p).wait_recv()
            add([peer, peer_twin], width if p else column_tile)
        whole = part[here].astype(jnp.bfloat16)
        summed[here] = whole
        error = (
            whole.astype(jnp.float32)
            + dec_bias_ref[...]
            - packed_targets[here].astype(jnp.float32)
        )
        live = jnp.concatenate([keep[here]] * (width // keep.shape[1]), axis=1)
        residual[here] = jnp.where(live > 0.0, error, 0.0).astype(jnp.bfloat16)

    load_live.wait()
    load_bias.wait()
    load_dec_bias.wait()
    load_act.wait()
    s1(1 - core).wait_recv()
    twin_tiles = live_ref[base + twin] + TILE - 1 >> 4
    for i in range(spare):
        own = core * block_tiles + sent - 1 - i
        theirs = (1 - core) * block_tiles + sent + i
        spill[spare - 1 - i] = acts_home[own + step(twin_tiles - sent - i) * (theirs - own)]
    for h in range(1, len(act_cuts)):
        s2(h).start()
    load_targets.wait()
    pack(acts_home, chip)
    load_enc.wait()
    encode(0)
    send(0)
    load_dec.wait()
    t1(twin, 0).wait_recv()
    home_features(0)

    for h in range(len(act_cuts)):
        s2(h).wait_recv()
    s3(core).start()
    s3(1 - core).wait_recv()
    pack(acts_away, other)
    encode(1)
    send(1)
    if rest:
        pack_rest()
        encode(2)
        send(2)
    for kind in kinds[1:]:
        t1(twin, kind).wait_recv()
        home_features(kind)
    for p in range(len(pieces)):
        finish(p)

    s1(core).wait_send()
    for h in range(len(act_cuts)):
        s2(h).wait_send()
    s3(core).wait_send()
    for kind in kinds:
        t1(me, kind).wait_send()
    for p in range(len(pieces)):
        t2(me, p, chip).wait_send()
        t3(peer, p).wait_send()


def choice_kernel(sizes, live_ref, choice_ref):
    choice = 0
    for group in range(0, live_ref.shape[0], 4):
        counts = [live_ref[group + b] + TILE - 1 >> 4 for b in range(4)]
        most = jnp.maximum(counts[0] + counts[1], counts[2] + counts[3])
        missed = sum(
            step(sum(counts) - tiles) | step(most - 2 * sent) for tiles, sent in sizes[:-1]
        )
        choice = jnp.maximum(choice, missed)
    choice_ref[0] = choice


def gradient_kernel(
    span,
    early,
    live_ref,
    codes_ref,
    residual_ref,
    summed_ref,
    bias_ref,
    rebuilt_hbm,
    grad_hbm,
    grad,
    rebuilt,
    sem,
):
    owners, width = codes_ref.shape[0], codes_ref.shape[2]
    block_tiles = rebuilt.shape[0] // TILE // 4
    base = lax.axis_index("blk") // 4 * 4
    per = width // span

    def out(f, i):
        at = pl.ds(pl.multiple_of(i * span, span), span)
        return pltpu.make_async_copy(grad.at[f, at], grad_hbm.at[f, at], sem.at[f * per + i])

    def block(f, i):
        at = pl.ds(i * span, span)
        grad[f, at] = lax.dot_general(
            codes_ref[f, :, at],
            residual_ref[...],
            (((0,), (0,)), ((), ())),
            preferred_element_type=jnp.float32,
        )
        out(f, i).start()

    counts = [live_ref[base + b] + TILE - 1 >> 4 for b in range(4)]
    first_extra = jnp.maximum(counts[0] + counts[1] - early // TILE, 0)

    def spread(b, s):
        live = live_ref[base + b]
        chip = b // 2
        k = b % 2 * (live_ref[base + b - b % 2] + TILE - 1 >> 4) + s
        place = jnp.where(
            k < early // TILE,
            chip * (early // TILE) + k,
            early // TILE + chip * first_extra + k,
        )
        place = jnp.where(TILE * s < live, place, 0)
        value = summed_ref[pl.ds(pl.multiple_of(place * TILE, TILE), TILE)].astype(jnp.float32)
        row = TILE * s + lax.broadcasted_iota(jnp.int32, value.shape, 0)
        at = pl.ds(pl.multiple_of((b * block_tiles + s) * TILE, TILE), TILE)
        rebuilt[at] = jnp.where(row < live, value, 0.0) + bias_ref[...]

    def give(b):
        at = pl.ds(pl.multiple_of(b * block_tiles * TILE, TILE), block_tiles * TILE)
        return pltpu.make_async_copy(rebuilt.at[at], rebuilt_hbm.at[at], sem.at[owners * per + b])

    def owner(f, carry):
        for i in range(per):
            block(f, i)
            for s in range(block_tiles * i // per, block_tiles * (i + 1) // per):
                spread(f, s)
        give(f).start()
        return carry

    lax.fori_loop(0, 4, owner, 0)

    def ended(i, carry):
        out(i // per, i % per).wait()
        return carry

    lax.fori_loop(0, owners * per, ended, 0)
    for b in range(4):
        give(b).wait()


def packed_tiles(
    order,
    tiles,
    sent,
    activations,
    live_rows,
    encoder_weight,
    encoder_bias,
    decoder_weight,
    decoder_bias,
    targets,
):
    rows, depth = activations.shape
    features = encoder_weight.shape[1]
    width = decoder_weight.shape[2]
    tokens = targets.shape[0]
    total = TILE * tiles
    early = total - 2 * rows
    block_tiles = rows // TILE
    spare = block_tiles - sent
    pieces = pieces_of(early, total - 2 * early)
    lanes = min(128, width)
    any_space = pl.BlockSpec(memory_space=pl.ANY)
    stay = functools.partial(pltpu.with_memory_space_constraint, memory_space=pltpu.HBM)
    in_vmem = pl.BlockSpec(memory_space=pltpu.VMEM)
    in_smem = pl.BlockSpec(memory_space=pltpu.SMEM)
    in_hbm = pl.BlockSpec(memory_space=pltpu.HBM)
    dma = pltpu.SemaphoreType.DMA
    bf16 = jnp.bfloat16
    f32 = jnp.float32
    codes, residual, summed = pl.pallas_call(
        functools.partial(gather_kernel, sent, early, pieces),
        out_shape=(
            pltpu.VMEM((4, total, features), bf16),
            pltpu.VMEM((total, width), bf16),
            pltpu.VMEM((total, width), bf16),
        ),
        in_specs=[in_hbm] * 7,
        out_specs=(in_vmem, in_vmem, in_vmem),
        scratch_shapes=[
            pltpu.VMEM((2 * block_tiles, TILE, depth), bf16),
            pltpu.VMEM((2 * sent, TILE, depth), bf16),
            pltpu.VMEM((max(spare, 1), TILE, depth), bf16),
            pltpu.VMEM((total, depth), bf16),
            pltpu.VMEM((depth, features), bf16),
            pltpu.VMEM((4, features, width), bf16),
            pltpu.VMEM((total, width), f32),
            pltpu.VMEM((4 * block_tiles, TILE, width), bf16),
            pltpu.VMEM((total, width), bf16),
            pltpu.VMEM((total, lanes), f32),
            pltpu.SMEM(live_rows.shape, jnp.int32),
            pltpu.VMEM((1, features), f32),
            pltpu.VMEM((1, width), f32),
            dma((7,)),
            dma((1,)),
            dma((1,)),
            dma((2,)),
            dma((2,)),
            dma((1,)),
            dma((1,)),
            dma((3,)),
            dma((3,)),
            dma((len(pieces),)),
            dma((len(pieces),)),
            dma((len(pieces),)),
            dma((len(pieces),)),
        ],
        compiler_params=pltpu.CompilerParams(
            collective_id=order, has_side_effects=True, vmem_limit_bytes=44 * 1024 * 1024
        ),
        name=f"gather_codes_{tiles}_{sent}",
    )(
        activations.reshape(block_tiles, TILE, depth),
        stay(live_rows),
        encoder_weight,
        stay(encoder_bias[None, :]),
        decoder_weight,
        stay(decoder_bias[None, :]),
        targets.reshape(4 * block_tiles, TILE, width),
    )

    span = min(256, features)
    rebuilt, grad = pl.pallas_call(
        functools.partial(gradient_kernel, span, early),
        out_shape=(
            jax.ShapeDtypeStruct((tokens, width), f32),
            jax.ShapeDtypeStruct((4, features, width), f32),
        ),
        in_specs=[in_smem, in_vmem, in_vmem, in_vmem, in_vmem],
        out_specs=(any_space, any_space),
        scratch_shapes=[
            pltpu.VMEM((4, features, width), f32),
            pltpu.VMEM((tokens, width), f32),
            dma((4 * (features // span) + 4,)),
        ],
        compiler_params=pltpu.CompilerParams(vmem_limit_bytes=44 * 1024 * 1024),
        name=f"gradient_{tiles}_{sent}",
    )(live_rows, codes, residual, summed, decoder_bias[None, :])
    return rebuilt, grad


def four_owners(activations, live_rows, *operands):
    rows = activations.shape[0]
    if rows % TILE:
        return general(activations, live_rows, *operands)
    block_tiles = rows // TILE
    fewer = max(block_tiles * 9 // 10, block_tiles // 2 + 1)
    shares = ((9, fewer), (12, fewer), (12, block_tiles), (15, block_tiles), (20, block_tiles))
    sizes = sorted({(2 * block_tiles + max(1, block_tiles * k // 10), sent) for k, sent in shares})
    in_smem = pl.BlockSpec(memory_space=pltpu.SMEM)
    choice = pl.pallas_call(
        functools.partial(choice_kernel, sizes),
        out_shape=pltpu.SMEM((1,), jnp.int32),
        in_specs=[in_smem],
        out_specs=in_smem,
        name="choice",
    )(live_rows)
    return lax.switch(
        choice[0],
        [functools.partial(packed_tiles, order, *size) for order, size in enumerate(sizes)],
        activations,
        live_rows,
        *operands,
    )


def from_partner(shard, axis, distance):
    return lax.ppermute(shard, axis, [(i, i ^ 1 << distance) for i in range(lax.axis_size(axis))])


def group_rows(block, levels, position):
    for bit in range(levels):
        other = from_partner(block, "blk", bit)
        upper = position >> bit & 1 == 1
        block = jnp.where(
            upper, jnp.concatenate([other, block], 0), jnp.concatenate([block, other], 0)
        )
    return block


def general(
    activations, live_rows, encoder_weight, encoder_bias, decoder_weight, decoder_bias, targets
):
    owners = lax.axis_size("blk") // G
    levels = owners.bit_length() - 1
    shares = lax.axis_size("feat")
    position = lax.axis_index("blk")
    share_index = lax.axis_index("feat")
    group_index = position // owners
    tok_rows = activations.shape[0]
    counts = lax.dynamic_slice_in_dim(live_rows, group_index * owners, owners)
    positions = jnp.arange(tok_rows, dtype=jnp.int32)
    live_mask = (positions[None, :] < counts[:, None]).astype(jnp.float32).reshape(-1)
    gathered = group_rows(activations, levels, position)
    per_share = encoder_weight.shape[1] // shares
    bias_share = lax.dynamic_slice_in_dim(encoder_bias, share_index * per_share, per_share)
    columns = encoder_weight
    whole = lax.psum(
        lax.dot_general(
            columns, gathered, (((0,), (1,)), ((), ())), preferred_element_type=jnp.float32
        ).astype(jnp.bfloat16),
        "feat",
    ).astype(jnp.float32)
    preact = lax.dynamic_slice_in_dim(whole, share_index * per_share, per_share, 0)
    codes_by_feature = (jax.nn.relu(preact + bias_share[:, None]) * live_mask[None, :]).astype(
        jnp.bfloat16
    )
    codes_all = group_rows(codes_by_feature, levels, position)
    decoder_rows = decoder_weight.reshape(-1, decoder_weight.shape[2])
    block_rows = gathered.shape[0] // shares
    columns = codes_all
    summed = lax.psum_scatter(
        lax.dot_general(
            columns, decoder_rows, (((0,), (0,)), ((), ())), preferred_element_type=jnp.float32
        ).astype(jnp.bfloat16),
        "feat",
        scatter_dimension=0,
        tiled=True,
    ).astype(jnp.float32)
    rebuilt = summed + decoder_bias[None, :]
    mask_block = lax.dynamic_slice_in_dim(live_mask, share_index * block_rows, block_rows)
    residual = ((rebuilt - targets.astype(jnp.float32)) * mask_block[:, None]).astype(jnp.bfloat16)
    columns = codes_all
    gradient = jnp.dot(
        columns,
        lax.all_gather(residual, "feat", axis=0, tiled=True),
        preferred_element_type=jnp.float32,
    )
    return (rebuilt, gradient.reshape(decoder_weight.shape))


def solution(mesh):
    in_specs = (
        P("blk", "feat"),
        P(),
        P("feat", "blk"),
        P("blk"),
        P(None, "feat", "blk"),
        P("blk"),
        P("feat", "blk"),
    )
    out_specs = (P("feat", "blk"), P(None, "feat", "blk"))
    fused = mesh.shape["blk"] // G == 4 and mesh.shape["feat"] == 1
    return jax.shard_map(
        four_owners if fused else general,
        mesh=mesh,
        in_specs=in_specs,
        out_specs=out_specs,
        check_vma=False,
    )
```
